512 devices in a mesh: energy: 64 (over x, y, core), cuts: 8 (over z).
Axes of the slice: x: 4, y: 8, z: 8, core: 2. Of those that a mesh axis runs over, the one named last changes fastest.
Arguments:
- g_lesser: float32 [2, 512, 8, 4096], P(None, 'energy', 'cuts'), may hold values from -6 to 6
- g_greater: float32 [2, 512, 8, 4096], P(None, 'energy', 'cuts'), may hold values from -6 to 6
- v_blocks: float32 [8, 64, 64], P('cuts'), may hold values from -0.75 to 0.75
- slots: int32 [8, 4096], P('cuts'), may hold values from 0 to 8191
Outputs:
- screened: float32 [2, 512, 8, 4096], P(None, 'energy', 'cuts')
The draws below stay inside these ranges and needn't reach their ends.
Inputs may be any that keep to these rules, and one draw needn't show every extreme that they name: slots[s, k] = row * 2 * 64 + column of element k of slice s, rows of the slice's orbitals, columns below 64 in the slice's own block and the others in its block towards the next slice; positions may repeat and then add.
All inputs are finite; a program needn't handle non-finite values.
Results may differ from the reference program's by a relative error of at most 0.0001.
Values sent between devices are 32-bit elements; how exact they have to be, the bound alone decides.
No kernel may reach another device: no remote copies, remote signals or barrier semaphores. Data moves between devices by JAX's collectives and lax.ppermute only.
A program may use at most 64 MiB of HBM per device.

```python
import math
import jax
import jax.numpy as jnp
from jax import lax

NE = 512
BLOCK = 64
NNZ = 4096
SLICES = 8


def touch_ends(values, rng, smallest, top_value):
    longest = values.shape.index(max(values.shape))
    spots = []
    for shift in (0, 1):
        where = [jax.random.randint(jax.random.fold_in(rng, axis), (), 0, length) for axis, length in enumerate(values.shape)]
        where[longest] = (where[longest] + shift) % values.shape[longest]
        spots.append(tuple(where))
    return values.at[spots[0]].set(smallest).at[spots[1]].set(top_value)


def levels(key, dims, split, smallest, high):
    def one(dim, blocks):
        steps = jax.random.uniform(jax.random.fold_in(jax.random.fold_in(key, 6), dim), (blocks,), jnp.float32, smallest / len(split), high / len(split))
        return jnp.repeat(jnp.exp(steps), dims[dim] // blocks).reshape((-1,) + (1,) * (len(dims) - dim - 1))

    level = one(*split[0])
    for cut in split[1:]:
        level = level * one(*cut)
    return level


def scatter_about(key, dims, deviation, reach, pieces=(), kind=jnp.bfloat16):
    level = levels(key, dims, pieces, -0.22, 0.18) if pieces else 1.0
    drawn = jax.random.normal(key, dims, jnp.float32) * deviation * level
    return jnp.minimum(jnp.maximum(drawn, -reach), reach).astype(kind)


def setup_inputs(seed: int = 0) -> dict:
    key_of = jax.random.split(jax.random.key(seed), 5)
    g_lesser = scatter_about(key_of[0], (2, NE, SLICES, NNZ), 1.0, 6.0, ((1, 64), (2, 8)), jnp.float32)
    g_greater = scatter_about(key_of[1], (2, NE, SLICES, NNZ), 1.0, 6.0, ((1, 64), (2, 8)), jnp.float32)
    v_blocks = scatter_about(key_of[2], (SLICES, BLOCK, BLOCK), BLOCK ** -0.5, 0.75, ((0, 8),), jnp.float32)
    slots = touch_ends(jax.random.randint(key_of[3], (SLICES, NNZ), 0, 2 * BLOCK * BLOCK), jax.random.fold_in(key_of[3], 1), 0, (2 * BLOCK * BLOCK) - 1).astype(jnp.int32)
    return {"g_lesser": g_lesser, "g_greater": g_greater, "v_blocks": v_blocks, "slots": slots}


SCREEN = 0.08
HIGHEST = lax.Precision.HIGHEST

def complex_product(first_matrix, second_matrix):
    real_part = jnp.einsum('...ij,...jk->...ik', first_matrix[0], second_matrix[0], precision=HIGHEST) - jnp.einsum('...ij,...jk->...ik', first_matrix[1], second_matrix[1], precision=HIGHEST)
    imag_part = jnp.einsum('...ij,...jk->...ik', first_matrix[0], second_matrix[1], precision=HIGHEST) + jnp.einsum('...ij,...jk->...ik', first_matrix[1], second_matrix[0], precision=HIGHEST)
    return jnp.stack([real_part, imag_part])

def correlate(inputs_pair):
    lesser, greater = inputs_pair
    energy_count = lesser.shape[1]
    padded_length = 2 * energy_count
    first_signal = lesser[0] + 1j * lesser[1]
    second_signal = greater[0] + 1j * greater[1]
    first_spectrum = jnp.fft.fft(first_signal, n=padded_length, axis=0)
    second_spectrum = jnp.fft.fft(second_signal, n=padded_length, axis=0)
    lagged = jnp.fft.ifft(first_spectrum * jnp.conj(second_spectrum), axis=0)[:energy_count]
    factor = 1.0 / math.sqrt(energy_count)
    return jnp.stack([-jnp.imag(lagged) * factor, jnp.real(lagged) * factor])

def reference(g_lesser, g_greater, v_blocks, slots):
    polar = lax.map(correlate, (jnp.moveaxis(g_lesser, 2, 0), jnp.moveaxis(g_greater, 2, 0)))
    polar = jnp.moveaxis(polar, 0, 2)
    block_width = 2 * BLOCK * BLOCK
    flat_index = (jnp.arange(SLICES, dtype=jnp.int32)[:, None] * block_width + slots).reshape(-1)
    dense = jnp.zeros((2, NE, SLICES * block_width), jnp.float32).at[:, :, flat_index].add(polar.reshape(2, NE, -1))
    dense = dense.reshape(2, NE, SLICES, BLOCK, 2 * BLOCK)
    diag_part = dense[..., :BLOCK]
    coupling = dense[..., BLOCK:]
    couple = SCREEN * jnp.einsum('sij,cesjk->cesik', v_blocks, coupling, precision=HIGHEST)
    source = jnp.einsum('sij,cesjk->cesik', v_blocks, diag_part, precision=HIGHEST)

    def advance(carried, inputs_pair):
        matrix, source_term = inputs_pair
        updated = complex_product(matrix, carried) + source_term
        return (updated, updated)
    initial = jnp.zeros((2, NE, BLOCK, BLOCK), jnp.float32)
    _, results = lax.scan(advance, initial, (jnp.moveaxis(couple, 2, 0), jnp.moveaxis(source, 2, 0)))
    return jnp.moveaxis(results, 0, 2).reshape(2, NE, SLICES, BLOCK * BLOCK)
```

```python
import functools
import math

import jax
import jax.numpy as jnp
import numpy as np
from jax import lax
from jax.experimental import pallas as pl
from jax.experimental.pallas import tpu as pltpu
from jax.sharding import PartitionSpec as P

SCREEN = 0.08
F32 = jnp.float32
BF16 = jnp.bfloat16
LANES = 128
HALF = 64


def split(x):
    high = x.astype(BF16)
    return high, (x - high.astype(F32)).astype(BF16)


def left_half(shape):
    return lax.broadcasted_iota(jnp.int32, shape, len(shape) - 1) < HALF


def dot(a, b):
    return jnp.dot(a, b, preferred_element_type=F32)


def pack_kernel(lesser_ref, greater_ref, out_ref):
    left = left_half((8, LANES))
    for tile in range(32):
        for which, ref in enumerate((lesser_ref, greater_ref)):
            real = ref[pl.ds(tile, 8, stride=32), :]
            imag = ref[pl.ds(256 + tile, 8, stride=32), :]
            rows = pl.ds(which * 8, 8)
            out_ref[2 * tile, rows, :] = jnp.where(left, real, pltpu.roll(imag, HALF, 1))
            out_ref[2 * tile + 1, rows, :] = jnp.where(left, pltpu.roll(real, HALF, 1), imag)


def correlate_kernel(data_ref, high_ref, low_ref, turn_ref, out_ref):
    count = 512
    lesser = data_ref[:, 0].reshape(count, LANES)
    greater = data_ref[:, 1].reshape(count, LANES)
    left = left_half((count, LANES))
    sign = jnp.where(left, 1.0, -1.0).astype(F32)

    def turned(x):
        return pltpu.roll(x, HALF, 1)

    signals = jnp.concatenate([lesser, greater], axis=1)
    sig_high, sig_low = split(signals)

    def transform(rows):
        table_high, table_low = high_ref[rows, :], low_ref[rows, :]
        return (
            dot(table_high, sig_high) + dot(table_high, sig_low) + dot(table_low, sig_high)
        )

    cosines = transform(pl.ds(0, count))
    sines = transform(pl.ds(count, count))
    cos_a, cos_b = cosines[:, :LANES], cosines[:, LANES:]
    sin_a, sin_b = sines[:, :LANES], sines[:, LANES:]
    shift_a, shift_b = sign * turned(sin_a), sign * turned(sin_b)

    def times_conjugate(a, b):
        other_b = turned(b)
        real_b = jnp.where(left, b, other_b)
        imag_b = jnp.where(left, other_b, b)
        return a * real_b + (sign * turned(a)) * imag_b

    plus = times_conjugate(cos_a + shift_a, cos_b + shift_b)
    minus = times_conjugate(cos_a - shift_a, cos_b - shift_b)
    for_cos = -sign * turned(plus + minus)
    for_sin = minus - plus
    turn_cos, turn_sin = turn_ref[0], turn_ref[1]
    cos_high, cos_low = split(turn_cos * for_cos - turn_sin * for_sin)
    sin_high, sin_low = split(turn_sin * for_cos + turn_cos * for_sin)
    cos_rows, sin_rows = pl.ds(0, count), pl.ds(count, count)
    result = dot(high_ref[cos_rows, :], cos_high) + dot(high_ref[sin_rows, :], sin_high)
    result += dot(high_ref[cos_rows, :], cos_low) + dot(high_ref[sin_rows, :], sin_low)
    result += dot(low_ref[cos_rows, :], cos_high) + dot(low_ref[sin_rows, :], sin_high)
    out_ref[...] = result


def repeated_row(ref, row):
    return jnp.broadcast_to(ref[pl.ds(row, 1), :], (16, LANES)).astype(BF16)


def screen_kernel(polar_ref, side_ref, out_ref, parts_ref, first_ref, second_ref, lines_ref, y_ref):
    left32 = left_half((32, LANES))
    row_iota = lax.broadcasted_iota(jnp.int32, (32, LANES), 0).astype(F32).astype(BF16)
    column_iota = lax.broadcasted_iota(jnp.int32, (256, LANES), 0).astype(F32).astype(BF16)
    zero = jnp.zeros((), BF16)
    one = jnp.ones((), BF16)

    def join(even, odd):
        return jnp.where(left32, even, pltpu.roll(odd, HALF, 1))

    def join_right(even, odd):
        return jnp.where(left32, pltpu.roll(even, HALF, 1), odd)

    def one_slice(s, carry):
        even = polar_ref[pl.ds(s, 32, stride=16), :]
        odd = polar_ref[pl.ds(s + 8, 32, stride=16), :]
        real_high, real_low = split(join(even, odd))
        imag_high, imag_low = split(join_right(even, odd))
        for i, part in enumerate((real_high, real_low, imag_high, imag_low)):
            parts_ref[i] = part.astype(F32)
        side = side_ref.at[s]
        slot = join_right(side[pl.ds(0, 32, stride=2), :], side[pl.ds(1, 32, stride=2), :])
        slot = slot.astype(jnp.int32)
        column = slot & 127
        moved = HALF + (column & 1) * 32 + ((column - HALF) >> 1)
        column = jnp.where(column < HALF, column, moved)
        lines_ref[0] = (slot >> 8).astype(F32)
        lines_ref[1] = ((slot & 128) + column).astype(F32)

        for r in range(32):
            lane = pl.ds(r * LANES, LANES)
            hit = jnp.concatenate([repeated_row(lines_ref.at[0], r)] * 2, axis=0) == row_iota
            for i in range(4):
                value = jnp.concatenate([repeated_row(parts_ref.at[i], r)] * 2, axis=0)
                first_ref[pl.ds(i * 32, 32), lane] = jnp.where(hit, value, zero)
            place = jnp.concatenate([repeated_row(lines_ref.at[1], r)] * 16, axis=0) == column_iota
            second_ref[:, lane] = jnp.where(place, one, zero)
        dense = lax.dot_general(
            first_ref[...], second_ref[...], (((1,), (1,)), ((), ())), preferred_element_type=F32
        )
        real = dense[0:32] + dense[32:64]
        imag = dense[64:96] + dense[96:128]
        dense = jnp.concatenate(
            [
                jnp.concatenate([real[:, :LANES], imag[:, :LANES]], axis=1),
                jnp.concatenate([real[:, LANES:], imag[:, LANES:]], axis=1),
            ],
            axis=0,
        )
        dense_high, dense_low = split(dense)
        v_high, v_low = split(side_ref[s][:, :HALF])
        y_ref[s] = dot(v_high, dense_high) + dot(v_high, dense_low) + dot(v_low, dense_high)
        return carry

    lax.fori_loop(0, 8, one_slice, 0)

    real = y_ref[0][:, :HALF]
    imag = y_ref[0][:, LANES : LANES + HALF]
    for s in range(8):
        y = y_ref[s]
        if s:
            couple_real = SCREEN * y[:, HALF:LANES]
            couple_imag = SCREEN * y[:, LANES + HALF :]
            matrix = jnp.concatenate(
                [
                    jnp.concatenate([couple_real, -couple_imag], axis=1),
                    jnp.concatenate([couple_imag, couple_real], axis=1),
                ],
                axis=0,
            )
            m_high, m_low = split(matrix)
            x_high, x_low = split(jnp.concatenate([real, imag], axis=0))
            product = dot(m_high, x_high) + dot(m_high, x_low) + dot(m_low, x_high)
            real = product[:HALF] + y[:, :HALF]
            imag = product[HALF:] + y[:, LANES : LANES + HALF]
        out_ref[s, 0] = jnp.concatenate([real[:32], real[32:]], axis=1)
        out_ref[s, 1] = jnp.concatenate([imag[:32], imag[32:]], axis=1)


def tables(count):
    half = np.arange(count) + 0.5
    angle = np.outer(half, half) * (math.pi / count)
    table = np.concatenate([np.cos(angle), np.sin(angle)]).astype(np.float32)
    high = table.astype(jnp.bfloat16)
    low = (table - high.astype(np.float32)).astype(jnp.bfloat16)
    turn = half * (math.pi / count) / 2
    scale = 1.0 / (2 * count * math.sqrt(count))
    turns = np.stack([np.cos(turn), np.sin(turn)]) * scale
    turns = np.broadcast_to(turns[:, :, None], (2, count, LANES)).astype(np.float32)
    return high, low, np.ascontiguousarray(turns)


def vmem(n):
    return [pl.BlockSpec(memory_space=pltpu.VMEM)] * n


def pack(lesser, greater):
    return pl.pallas_call(
        pack_kernel,
        out_shape=jax.ShapeDtypeStruct((64, 16, LANES), F32),
        in_specs=vmem(2),
        out_specs=vmem(1)[0],
        name="pack",
    )(lesser.reshape(512, LANES), greater.reshape(512, LANES))


def correlate(data):
    high, low, turns = tables(512)
    return pl.pallas_call(
        correlate_kernel,
        out_shape=jax.ShapeDtypeStruct((512, LANES), F32),
        in_specs=vmem(4),
        out_specs=vmem(1)[0],
        compiler_params=pltpu.CompilerParams(vmem_limit_bytes=40 << 20),
        name="correlate",
    )(data.reshape(64, 2, 8, LANES), jnp.asarray(high), jnp.asarray(low), jnp.asarray(turns))


def screen(polar, side):
    return pl.pallas_call(
        screen_kernel,
        out_shape=jax.ShapeDtypeStruct((8, 2, 32, LANES), F32),
        in_specs=vmem(2),
        out_specs=vmem(1)[0],
        scratch_shapes=[
            pltpu.VMEM((4, 32, LANES), F32),
            pltpu.VMEM((LANES, 4096), BF16),
            pltpu.VMEM((256, 4096), BF16),
            pltpu.VMEM((2, 32, LANES), F32),
            pltpu.VMEM((8, HALF, 256), F32),
        ],
        compiler_params=pltpu.CompilerParams(vmem_limit_bytes=40 << 20),
        name="screen",
    )(polar, side)


def side_rows(v_blocks, slots):
    v = v_blocks.reshape(32, 2, 32, 2).transpose(1, 0, 3, 2).reshape(HALF, HALF)
    return jnp.concatenate([v, slots.reshape(HALF, HALF).astype(F32)], axis=1)


def shards(g_lesser, g_greater, v_blocks, slots):
    side = lax.all_gather(side_rows(v_blocks, slots), "cuts")
    data = lax.all_to_all(pack(g_lesser, g_greater), "energy", 0, 0, tiled=True)
    polar = correlate(data)
    polar = lax.all_to_all(
        polar.reshape(512, 1, LANES), ("energy", "cuts"), 0, 0, tiled=True
    ).reshape(512, LANES)
    blocks = screen(polar, side).reshape(8, 64, LANES)
    blocks = lax.all_to_all(blocks, "cuts", 0, 0, tiled=True)
    return blocks.reshape(8, 2, 4096).transpose(1, 0, 2).reshape(2, 8, 1, 4096)


def solution(mesh):
    placed = (
        P(None, "energy", "cuts", None),
        P(None, "energy", "cuts", None),
        P("cuts", None, None),
        P("cuts", None),
    )
    return jax.shard_map(
        shards,
        mesh=mesh,
        in_specs=placed,
        out_specs=P(None, "energy", "cuts", None),
        check_vma=False,
    )
```

```python
import functools
import math

import jax
import jax.numpy as jnp
import numpy as np
from jax import lax
from jax.experimental import pallas as pl
from jax.experimental.pallas import tpu as pltpu
from jax.sharding import PartitionSpec as P

SCREEN = 0.08
F32 = jnp.float32
BF16 = jnp.bfloat16
LANES = 128
HALF = 64
SIDE = 256


def split(x):
    high = x.astype(BF16)
    return high, (x - high.astype(F32)).astype(BF16)


def left_half(shape):
    return lax.broadcasted_iota(jnp.int32, shape, len(shape) - 1) < HALF


def dot(a, b):
    return jnp.dot(a, b, preferred_element_type=F32)


def pack_kernel(lesser_ref, greater_ref, v_ref, slots_ref, out_ref, side_ref):
    side_ref[pl.ds(0, 32), :] = slots_ref[...].astype(F32)
    side_ref[pl.ds(32, HALF), :] = jnp.concatenate([v_ref[0], v_ref[0]], axis=1)
    side_ref[pl.ds(96, SIDE - 96), :] = jnp.zeros((SIDE - 96, LANES), F32)
    left = left_half((8, LANES))
    for tile in range(32):
        for which, ref in enumerate((lesser_ref, greater_ref)):
            real = ref[pl.ds(tile, 8, stride=32), :]
            imag = ref[pl.ds(256 + tile, 8, stride=32), :]
            rows = pl.ds(which * 8, 8)
            out_ref[2 * tile, rows, :] = jnp.where(left, real, pltpu.roll(imag, HALF, 1))
            out_ref[2 * tile + 1, rows, :] = jnp.where(left, pltpu.roll(real, HALF, 1), imag)


def correlate_kernel(data_ref, table_ref, out_ref):
    count = 512
    high_ref, low_ref = table_ref.at[pl.ds(0, 2 * count)], table_ref.at[pl.ds(2 * count, 2 * count)]
    lesser = data_ref[:, 0].reshape(count, LANES)
    greater = data_ref[:, 1].reshape(count, LANES)
    left = left_half((count, LANES))
    sign = jnp.where(left, 1.0, -1.0).astype(F32)

    def turned(x):
        return pltpu.roll(x, HALF, 1)

    signals = jnp.concatenate([lesser, greater], axis=1)
    sig_high, sig_low = split(signals)

    def transform(rows):
        table_high, table_low = high_ref[rows, :], low_ref[rows, :]
        return (
            dot(table_high, sig_high) + dot(table_high, sig_low) + dot(table_low, sig_high)
        )

    cosines = transform(pl.ds(0, count))
    sines = transform(pl.ds(count, count))
    cos_a, cos_b = cosines[:, :LANES], cosines[:, LANES:]
    sin_a, sin_b = sines[:, :LANES], sines[:, LANES:]
    shift_a, shift_b = sign * turned(sin_a), sign * turned(sin_b)

    def times_conjugate(a, b):
        other_b = turned(b)
        real_b = jnp.where(left, b, other_b)
        imag_b = jnp.where(left, other_b, b)
        return a * real_b + (sign * turned(a)) * imag_b

    plus = times_conjugate(cos_a + shift_a, cos_b + shift_b)
    minus = times_conjugate(cos_a - shift_a, cos_b - shift_b)
    for_cos = -sign * turned(plus + minus)
    for_sin = minus - plus
    scale = 1.0 / (2 * count * math.sqrt(count))

    def turn(rows):
        column = high_ref[rows, :LANES][:, :1].astype(F32) + low_ref[rows, :LANES][:, :1].astype(F32)
        return jnp.broadcast_to(column * scale, (count, LANES))

    turn_cos, turn_sin = turn(pl.ds(0, count)), turn(pl.ds(count, count))
    cos_high, cos_low = split(turn_cos * for_cos - turn_sin * for_sin)
    sin_high, sin_low = split(turn_sin * for_cos + turn_cos * for_sin)
    cos_rows, sin_rows = pl.ds(0, count), pl.ds(count, count)
    result = dot(high_ref[cos_rows, :], cos_high) + dot(high_ref[sin_rows, :], sin_high)
    result += dot(high_ref[cos_rows, :], cos_low) + dot(high_ref[sin_rows, :], sin_low)
    result += dot(low_ref[cos_rows, :], cos_high) + dot(low_ref[sin_rows, :], sin_high)
    out_ref[...] = result


def repeated_row(ref, row):
    return jnp.broadcast_to(ref[pl.ds(row, 1), :], (16, LANES)).astype(BF16)


def screen_kernel(polar_ref, side_ref, out_ref, parts_ref, first_ref, second_ref, lines_ref, y_ref):
    left32 = left_half((32, LANES))
    row_iota = lax.broadcasted_iota(jnp.int32, (32, LANES), 0).astype(F32).astype(BF16)
    column_iota = lax.broadcasted_iota(jnp.int32, (256, LANES), 0).astype(F32).astype(BF16)
    zero = jnp.zeros((), BF16)
    one = jnp.ones((), BF16)

    def join(even, odd):
        return jnp.where(left32, even, pltpu.roll(odd, HALF, 1))

    def join_right(even, odd):
        return jnp.where(left32, pltpu.roll(even, HALF, 1), odd)

    def one_slice(s, carry):
        even = polar_ref[pl.ds(s, 32, stride=16), :]
        odd = polar_ref[pl.ds(s + 8, 32, stride=16), :]
        real_high, real_low = split(join(even, odd))
        imag_high, imag_low = split(join_right(even, odd))
        for i, part in enumerate((real_high, real_low, imag_high, imag_low)):
            parts_ref[i] = part.astype(F32)
        side = side_ref.at[s]
        slot = side[pl.ds(0, 32), :].astype(jnp.int32)
        column = slot & 127
        moved = HALF + (column & 1) * 32 + ((column - HALF) >> 1)
        column = jnp.where(column < HALF, column, moved)
        lines_ref[0] = ((slot >> 7) & 31).astype(F32)
        lines_ref[1] = (((slot >> 12) << 7) + column).astype(F32)

        for r in range(32):
            lane = pl.ds(r * LANES, LANES)
            hit = jnp.concatenate([repeated_row(lines_ref.at[0], r)] * 2, axis=0) == row_iota
            for i in range(4):
                value = jnp.concatenate([repeated_row(parts_ref.at[i], r)] * 2, axis=0)
                first_ref[pl.ds(i * 32, 32), lane] = jnp.where(hit, value, zero)
            place = jnp.concatenate([repeated_row(lines_ref.at[1], r)] * 16, axis=0) == column_iota
            second_ref[:, lane] = jnp.where(place, one, zero)
        dense = lax.dot_general(
            first_ref[...], second_ref[...], (((1,), (1,)), ((), ())), preferred_element_type=F32
        )
        real = dense[0:32] + dense[32:64]
        imag = dense[64:96] + dense[96:128]
        dense = jnp.concatenate(
            [
                jnp.concatenate([real[:, :LANES], imag[:, :LANES]], axis=1),
                jnp.concatenate([real[:, LANES:], imag[:, LANES:]], axis=1),
            ],
            axis=0,
        )
        dense_high, dense_low = split(dense)
        rows = [side[pl.ds(32 + parity, 32, stride=2), :] for parity in range(2)]
        v_high, v_low = split(jnp.concatenate(rows, axis=0)[:, :HALF])
        y_ref[s] = dot(v_high, dense_high) + dot(v_high, dense_low) + dot(v_low, dense_high)
        return carry

    lax.fori_loop(0, 8, one_slice, 0)

    real = y_ref[0][:, :HALF]
    imag = y_ref[0][:, LANES : LANES + HALF]
    for s in range(8):
        y = y_ref[s]
        if s:
            couple_real = SCREEN * y[:, HALF:LANES]
            couple_imag = SCREEN * y[:, LANES + HALF :]
            matrix = jnp.concatenate(
                [
                    jnp.concatenate([couple_real, -couple_imag], axis=1),
                    jnp.concatenate([couple_imag, couple_real], axis=1),
                ],
                axis=0,
            )
            m_high, m_low = split(matrix)
            x_high, x_low = split(jnp.concatenate([real, imag], axis=0))
            product = dot(m_high, x_high) + dot(m_high, x_low) + dot(m_low, x_high)
            real = product[:HALF] + y[:, :HALF]
            imag = product[HALF:] + y[:, LANES : LANES + HALF]
        out_ref[s, 0] = jnp.concatenate([real[:32], real[32:]], axis=1)
        out_ref[s, 1] = jnp.concatenate([imag[:32], imag[32:]], axis=1)


def tables(count):
    half = np.arange(count) + 0.5
    angle = np.outer(half, half) * (math.pi / count)
    table = np.concatenate([np.cos(angle), np.sin(angle)]).astype(np.float32)
    high = table.astype(jnp.bfloat16)
    low = (table - high.astype(np.float32)).astype(jnp.bfloat16)
    return np.concatenate([high, low])


def vmem(n):
    return [pl.BlockSpec(memory_space=pltpu.VMEM)] * n


def pack(lesser, greater, v_blocks, slots):
    return pl.pallas_call(
        pack_kernel,
        out_shape=(
            jax.ShapeDtypeStruct((64, 16, LANES), F32),
            jax.ShapeDtypeStruct((SIDE, LANES), F32),
        ),
        in_specs=vmem(4),
        out_specs=tuple(vmem(2)),
        name="pack",
    )(
        lesser.reshape(512, LANES),
        greater.reshape(512, LANES),
        v_blocks,
        slots.reshape(32, LANES),
    )


def correlate(data):
    return pl.pallas_call(
        correlate_kernel,
        out_shape=jax.ShapeDtypeStruct((512, LANES), F32),
        in_specs=vmem(2),
        out_specs=vmem(1)[0],
        compiler_params=pltpu.CompilerParams(vmem_limit_bytes=40 << 20),
        name="correlate",
    )(data.reshape(64, 2, 8, LANES), jnp.asarray(tables(512)))


def screen(polar, side):
    return pl.pallas_call(
        screen_kernel,
        out_shape=jax.ShapeDtypeStruct((8, 2, 32, LANES), F32),
        in_specs=vmem(2),
        out_specs=vmem(1)[0],
        scratch_shapes=[
            pltpu.VMEM((4, 32, LANES), F32),
            pltpu.VMEM((LANES, 4096), BF16),
            pltpu.VMEM((256, 4096), BF16),
            pltpu.VMEM((2, 32, LANES), F32),
            pltpu.VMEM((8, HALF, 256), F32),
        ],
        compiler_params=pltpu.CompilerParams(vmem_limit_bytes=40 << 20),
        name="screen",
    )(polar, side)


def shards(g_lesser, g_greater, v_blocks, slots):
    data, side = pack(g_lesser, g_greater, v_blocks, slots)
    side = lax.all_gather(side, "cuts")
    data = lax.all_to_all(data, "energy", 0, 0, tiled=True)
    polar = correlate(data)
    polar = lax.all_to_all(
        polar.reshape(512, 1, LANES), ("energy", "cuts"), 0, 0, tiled=True
    ).reshape(512, LANES)
    blocks = screen(polar, side).reshape(8, 64, LANES)
    blocks = lax.all_to_all(blocks, "cuts", 0, 0, tiled=True)
    return blocks.reshape(8, 2, 4096).transpose(1, 0, 2).reshape(2, 8, 1, 4096)


def solution(mesh):
    placed = (
        P(None, "energy", "cuts", None),
        P(None, "energy", "cuts", None),
        P("cuts", None, None),
        P("cuts", None),
    )
    return jax.shard_map(
        shards,
        mesh=mesh,
        in_specs=placed,
        out_specs=P(None, "energy", "cuts", None),
        check_vma=False,
    )
```

```python
import functools
import math

import jax
import jax.numpy as jnp
import numpy as np
from jax import lax
from jax.experimental import pallas as pl
from jax.experimental.pallas import tpu as pltpu
from jax.sharding import PartitionSpec as P

SCREEN = 0.08
F32 = jnp.float32
BF16 = jnp.bfloat16
LANES = 128
HALF = 64


def split(x):
    high = x.astype(BF16)
    return high, (x - high.astype(F32)).astype(BF16)


def left_half(shape):
    return lax.broadcasted_iota(jnp.int32, shape, len(shape) - 1) < HALF


def dot(a, b):
    return jnp.dot(a, b, preferred_element_type=F32)


def pack_kernel(lesser_ref, greater_ref, out_ref):
    left = left_half((8, LANES))
    for tile in range(32):
        for which, ref in enumerate((lesser_ref, greater_ref)):
            real = ref[pl.ds(tile, 8, stride=32), :]
            imag = ref[pl.ds(256 + tile, 8, stride=32), :]
            rows = pl.ds(which * 8, 8)
            out_ref[2 * tile, rows, :] = jnp.where(left, real, pltpu.roll(imag, HALF, 1))
            out_ref[2 * tile + 1, rows, :] = jnp.where(left, pltpu.roll(real, HALF, 1), imag)


def correlate_kernel(data_ref, v_ref, slots_ref, table_hbm, out_ref, table_ref, sems):
    count = 512
    copies = []
    for i in range(4):
        rows = pl.ds(i * count, count)
        copies.append(pltpu.make_async_copy(table_hbm.at[rows], table_ref.at[i], sems.at[i]))
        copies[i].start()
    left = left_half((count, LANES))
    sign = jnp.where(left, 1.0, -1.0).astype(F32)

    def turned(x):
        return pltpu.roll(x, HALF, 1)

    me = lax.axis_index("energy")
    slot = slots_ref[pl.ds(me // 2, 1), :].astype(F32)
    slot = jnp.where(me % 2 == 0, slot, turned(slot))[:, :HALF]
    side = jnp.concatenate([slot, v_ref[0, pl.ds(me, 1), :]], axis=1)
    out_ref[pl.ds(1, count, stride=2), :] = jnp.broadcast_to(side, (count, LANES))

    lesser = data_ref[:, 0].reshape(count, LANES)
    greater = data_ref[:, 1].reshape(count, LANES)
    sig_high, sig_low = split(jnp.concatenate([lesser, greater], axis=1))
    both = jnp.concatenate([sig_high, sig_low], axis=1)
    copies[0].wait()
    cosines = dot(table_ref[0], both)
    copies[1].wait()
    sines = dot(table_ref[1], both)
    copies[2].wait()
    cosines = cosines[:, :256] + cosines[:, 256:] + dot(table_ref[2], sig_high)
    copies[3].wait()
    sines = sines[:, :256] + sines[:, 256:] + dot(table_ref[3], sig_high)
    cos_a, cos_b = cosines[:, :LANES], cosines[:, LANES:]
    sin_a, sin_b = sines[:, :LANES], sines[:, LANES:]
    shift_a, shift_b = sign * turned(sin_a), sign * turned(sin_b)

    def times_conjugate(a, b):
        other_b = turned(b)
        real_b = jnp.where(left, b, other_b)
        imag_b = jnp.where(left, other_b, b)
        return a * real_b + (sign * turned(a)) * imag_b

    plus = times_conjugate(cos_a + shift_a, cos_b + shift_b)
    minus = times_conjugate(cos_a - shift_a, cos_b - shift_b)
    for_cos = -sign * turned(plus + minus)
    for_sin = minus - plus
    scale = 1.0 / (2 * count * math.sqrt(count))

    def turn(i):
        column = table_ref[i, :, :LANES][:, :1].astype(F32)
        column += table_ref[i + 2, :, :LANES][:, :1].astype(F32)
        return jnp.broadcast_to(column * scale, (count, LANES))

    turn_cos, turn_sin = turn(0), turn(1)
    cos_high, cos_low = split(turn_cos * for_cos - turn_sin * for_sin)
    sin_high, sin_low = split(turn_sin * for_cos + turn_cos * for_sin)
    result = dot(table_ref[0], jnp.concatenate([cos_high, cos_low], axis=1))
    result += dot(table_ref[1], jnp.concatenate([sin_high, sin_low], axis=1))
    result = result[:, :LANES] + result[:, LANES:]
    result += dot(table_ref[2], cos_high) + dot(table_ref[3], sin_high)
    out_ref[pl.ds(0, count, stride=2), :] = result


def repeated_row(ref, row, times):
    tile = jnp.broadcast_to(ref[pl.ds(row, 1), :], (16, LANES)).astype(BF16)
    return jnp.concatenate([tile] * times, axis=0)


def screen_kernel(data_ref, out_ref, parts_ref, lines_ref, dense_ref):
    left32 = left_half((32, LANES))
    row_iota = lax.broadcasted_iota(jnp.int32, (HALF, LANES), 0).astype(F32).astype(BF16)
    column_iota = lax.broadcasted_iota(jnp.int32, (LANES, LANES), 0).astype(F32).astype(BF16)
    zero = jnp.zeros((), BF16)
    one = jnp.ones((), BF16)

    def lines(s, side):
        return [data_ref[pl.ds(2 * s + side + 16 * odd, 32, stride=32), :] for odd in range(2)]

    def join(even, odd):
        return jnp.where(left32, even, pltpu.roll(odd, HALF, 1))

    def join_right(even, odd):
        return jnp.where(left32, pltpu.roll(even, HALF, 1), odd)

    def v_rows(s):
        return jnp.concatenate(lines(s, 1), axis=0)[:, HALF:]

    def one_slice(s, carry):
        polar = lines(s, 0)
        for i, part in enumerate((*split(join(*polar)), *split(join_right(*polar)))):
            parts_ref[i] = part.astype(F32)
        slot = join(*lines(s, 1)).astype(jnp.int32)
        column = slot & 127
        moved = HALF + (column & 1) * 32 + ((column - HALF) >> 1)
        lines_ref[0] = (slot >> 7).astype(F32)
        lines_ref[1] = jnp.where(column < HALF, column, moved).astype(F32)

        def chunk(r):
            hit = repeated_row(lines_ref.at[0], r, 4) == row_iota
            first = [jnp.where(hit, repeated_row(parts_ref.at[i], r, 4), zero) for i in range(4)]
            place = repeated_row(lines_ref.at[1], r, 8) == column_iota
            return jnp.concatenate(first, axis=0), jnp.where(place, one, zero)

        dense = None
        for r in range(0, 32, 2):
            pairs = [chunk(r), chunk(r + 1)]
            first = jnp.concatenate([pair[0] for pair in pairs], axis=1)
            second = jnp.concatenate([pair[1] for pair in pairs], axis=1)
            term = lax.dot_general(
                first, second, (((1,), (1,)), ((), ())), preferred_element_type=F32
            )
            dense = term if dense is None else dense + term
        real = dense[0:64] + dense[64:128]
        imag = dense[128:192] + dense[192:256]
        dense_ref[s] = jnp.concatenate([real, imag], axis=1)
        return carry

    lax.fori_loop(0, 8, one_slice, 0)

    y = []
    for s in range(8):
        high, low = split(dense_ref[s])
        v_high, v_low = split(v_rows(s))
        y.append(dot(v_high, high) + dot(v_high, low) + dot(v_low, high))
    for s in range(8):
        source_real, source_imag = y[s][:, :HALF], y[s][:, LANES : LANES + HALF]
        if s == 0:
            real, imag = source_real, source_imag
        else:
            couple_real = SCREEN * y[s][:, HALF:LANES]
            couple_imag = SCREEN * y[s][:, LANES + HALF :]
            matrix = jnp.concatenate(
                [
                    jnp.concatenate([couple_real, -couple_imag], axis=1),
                    jnp.concatenate([couple_imag, couple_real], axis=1),
                ],
                axis=0,
            )
            m_high, m_low = split(matrix)
            x_high, x_low = split(jnp.concatenate([real, imag], axis=0))
            product = dot(m_high, x_high) + dot(m_high, x_low) + dot(m_low, x_high)
            real = product[:HALF] + source_real
            imag = product[HALF:] + source_imag
        out_ref[s, 0] = jnp.concatenate([real[:32], real[32:]], axis=1)
        out_ref[s, 1] = jnp.concatenate([imag[:32], imag[32:]], axis=1)


def tables(count):
    half = np.arange(count) + 0.5
    angle = np.outer(half, half) * (math.pi / count)
    table = np.concatenate([np.cos(angle), np.sin(angle)]).astype(np.float32)
    high = table.astype(jnp.bfloat16)
    low = (table - high.astype(np.float32)).astype(jnp.bfloat16)
    return np.concatenate([high, low])


def vmem(n):
    return [pl.BlockSpec(memory_space=pltpu.VMEM)] * n


def pack(lesser, greater):
    return pl.pallas_call(
        pack_kernel,
        out_shape=jax.ShapeDtypeStruct((64, 16, LANES), F32),
        in_specs=vmem(2),
        out_specs=vmem(1)[0],
        name="pack",
    )(lesser.reshape(512, LANES), greater.reshape(512, LANES))


def correlate(data, v_blocks, slots):
    return pl.pallas_call(
        correlate_kernel,
        out_shape=jax.ShapeDtypeStruct((1024, LANES), F32),
        in_specs=vmem(3) + [pl.BlockSpec(memory_space=pl.ANY)],
        out_specs=vmem(1)[0],
        scratch_shapes=[pltpu.VMEM((4, 512, 512), BF16), pltpu.SemaphoreType.DMA((4,))],
        compiler_params=pltpu.CompilerParams(vmem_limit_bytes=40 << 20),
        name="correlate",
    )(data.reshape(64, 2, 8, LANES), v_blocks, slots.reshape(32, LANES), jnp.asarray(tables(512)))


def screen(data):
    return pl.pallas_call(
        screen_kernel,
        out_shape=jax.ShapeDtypeStruct((8, 2, 32, LANES), F32),
        in_specs=vmem(1),
        out_specs=vmem(1)[0],
        scratch_shapes=[
            pltpu.VMEM((4, 32, LANES), F32),
            pltpu.VMEM((2, 32, LANES), F32),
            pltpu.VMEM((8, HALF, 256), F32),
        ],
        compiler_params=pltpu.CompilerParams(vmem_limit_bytes=40 << 20),
        name="screen",
    )(data)


def shards(g_lesser, g_greater, v_blocks, slots):
    data = lax.all_to_all(pack(g_lesser, g_greater), "energy", 0, 0, tiled=True)
    data = correlate(data, v_blocks, slots).reshape(512, 1, 256)
    data = lax.all_to_all(data, ("energy", "cuts"), 0, 0, tiled=True)
    blocks = screen(data.reshape(1024, LANES)).reshape(8, 64, LANES)
    blocks = lax.all_to_all(blocks, "cuts", 0, 0, tiled=True)
    return blocks.reshape(8, 2, 4096).transpose(1, 0, 2).reshape(2, 8, 1, 4096)


def solution(mesh):
    placed = (
        P(None, "energy", "cuts", None),
        P(None, "energy", "cuts", None),
        P("cuts", None, None),
        P("cuts", None),
    )
    return jax.shard_map(
        shards,
        mesh=mesh,
        in_specs=placed,
        out_specs=P(None, "energy", "cuts", None),
        check_vma=False,
    )
```

```python
import functools
import math

import jax
import jax.numpy as jnp
import numpy as np
from jax import lax
from jax.experimental import pallas as pl
from jax.experimental.pallas import tpu as pltpu
from jax.sharding import PartitionSpec as P

SCREEN = 0.08
F32 = jnp.float32
BF16 = jnp.bfloat16
LANES = 128
HALF = 64


def split(x):
    high = x.astype(BF16)
    return high, (x - high.astype(F32)).astype(BF16)


def left_half(shape):
    return lax.broadcasted_iota(jnp.int32, shape, len(shape) - 1) < HALF


def dot(a, b):
    return jnp.dot(a, b, preferred_element_type=F32)


def pack_kernel(
    lesser_ref, greater_ref, v_ref, slots_ref, table_hbm, out_ref, side_ref, table_ref, sem
):
    copy = pltpu.make_async_copy(table_hbm, table_ref, sem)
    copy.start()
    me = lax.axis_index("energy")
    slot = slots_ref[pl.ds(me // 2, 1), :].astype(F32)
    slot = jnp.where(me % 2 == 0, slot, pltpu.roll(slot, HALF, 1))[:, :HALF]
    side = jnp.concatenate([slot, v_ref[0, pl.ds(me, 1), :]], axis=1)
    side_ref[...] = jnp.broadcast_to(side, (8, LANES))
    left = left_half((8, LANES))
    for tile in range(32):
        for which, ref in enumerate((lesser_ref, greater_ref)):
            real = ref[pl.ds(tile, 8, stride=32), :]
            imag = ref[pl.ds(256 + tile, 8, stride=32), :]
            rows = pl.ds(which * 8, 8)
            out_ref[2 * tile, rows, :] = jnp.where(left, real, pltpu.roll(imag, HALF, 1))
            out_ref[2 * tile + 1, rows, :] = jnp.where(left, pltpu.roll(real, HALF, 1), imag)
    copy.wait()


def correlate_kernel(data_ref, side_ref, table_ref, out_ref):
    count = 512
    left = left_half((count, LANES))
    sign = jnp.where(left, 1.0, -1.0).astype(F32)

    def turned(x):
        return pltpu.roll(x, HALF, 1)

    out_ref[pl.ds(1, count, stride=2), :] = jnp.broadcast_to(side_ref[pl.ds(0, 1), :], (count, LANES))

    lesser = data_ref[:, 0].reshape(count, LANES)
    greater = data_ref[:, 1].reshape(count, LANES)
    sig_high, sig_low = split(jnp.concatenate([lesser, greater], axis=1))
    both = jnp.concatenate([sig_high, sig_low], axis=1)
    cosines = dot(table_ref[0], both)
    sines = dot(table_ref[1], both)
    cosines = cosines[:, :256] + cosines[:, 256:] + dot(table_ref[2], sig_high)
    sines = sines[:, :256] + sines[:, 256:] + dot(table_ref[3], sig_high)
    cos_a, cos_b = cosines[:, :LANES], cosines[:, LANES:]
    sin_a, sin_b = sines[:, :LANES], sines[:, LANES:]
    shift_a, shift_b = sign * turned(sin_a), sign * turned(sin_b)

    def times_conjugate(a, b):
        other_b = turned(b)
        real_b = jnp.where(left, b, other_b)
        imag_b = jnp.where(left, other_b, b)
        return a * real_b + (sign * turned(a)) * imag_b

    plus = times_conjugate(cos_a + shift_a, cos_b + shift_b)
    minus = times_conjugate(cos_a - shift_a, cos_b - shift_b)
    for_cos = -sign * turned(plus + minus)
    for_sin = minus - plus
    scale = 1.0 / (2 * count * math.sqrt(count))

    def turn(i):
        column = table_ref[i, :, :LANES][:, :1].astype(F32)
        column += table_ref[i + 2, :, :LANES][:, :1].astype(F32)
        return jnp.broadcast_to(column * scale, (count, LANES))

    turn_cos, turn_sin = turn(0), turn(1)
    cos_high, cos_low = split(turn_cos * for_cos - turn_sin * for_sin)
    sin_high, sin_low = split(turn_sin * for_cos + turn_cos * for_sin)
    result = dot(table_ref[0], jnp.concatenate([cos_high, cos_low], axis=1))
    result += dot(table_ref[1], jnp.concatenate([sin_high, sin_low], axis=1))
    result = result[:, :LANES] + result[:, LANES:]
    result += dot(table_ref[2], cos_high) + dot(table_ref[3], sin_high)
    out_ref[pl.ds(0, count, stride=2), :] = result


def repeated_row(ref, row, times):
    tile = jnp.broadcast_to(ref[pl.ds(row, 1), :], (16, LANES)).astype(BF16)
    return jnp.concatenate([tile] * times, axis=0)


def screen_kernel(data_ref, out_ref, parts_ref, lines_ref, dense_ref):
    left32 = left_half((32, LANES))
    row_iota = lax.broadcasted_iota(jnp.int32, (HALF, LANES), 0).astype(F32).astype(BF16)
    column_iota = lax.broadcasted_iota(jnp.int32, (LANES, LANES), 0).astype(F32).astype(BF16)
    zero = jnp.zeros((), BF16)
    one = jnp.ones((), BF16)

    def lines(s, side):
        return [data_ref[pl.ds(2 * s + side + 16 * odd, 32, stride=32), :] for odd in range(2)]

    def join(even, odd):
        return jnp.where(left32, even, pltpu.roll(odd, HALF, 1))

    def join_right(even, odd):
        return jnp.where(left32, pltpu.roll(even, HALF, 1), odd)

    def v_rows(s):
        return jnp.concatenate(lines(s, 1), axis=0)[:, HALF:]

    def one_slice(s, carry):
        polar = lines(s, 0)
        for i, part in enumerate((*split(join(*polar)), *split(join_right(*polar)))):
            parts_ref[i] = part.astype(F32)
        slot = join(*lines(s, 1)).astype(jnp.int32)
        column = slot & 127
        moved = HALF + (column & 1) * 32 + ((column - HALF) >> 1)
        lines_ref[0] = (slot >> 7).astype(F32)
        lines_ref[1] = jnp.where(column < HALF, column, moved).astype(F32)

        def chunk(r):
            hit = repeated_row(lines_ref.at[0], r, 4) == row_iota
            first = [jnp.where(hit, repeated_row(parts_ref.at[i], r, 4), zero) for i in range(4)]
            place = repeated_row(lines_ref.at[1], r, 8) == column_iota
            return jnp.concatenate(first, axis=0), jnp.where(place, one, zero)

        dense = None
        for r in range(0, 32, 2):
            pairs = [chunk(r), chunk(r + 1)]
            first = jnp.concatenate([pair[0] for pair in pairs], axis=1)
            second = jnp.concatenate([pair[1] for pair in pairs], axis=1)
            term = lax.dot_general(
                first, second, (((1,), (1,)), ((), ())), preferred_element_type=F32
            )
            dense = term if dense is None else dense + term
        real = dense[0:64] + dense[64:128]
        imag = dense[128:192] + dense[192:256]
        dense_ref[s] = jnp.concatenate([real, imag], axis=1)
        return carry

    lax.fori_loop(0, 8, one_slice, 0)

    y = []
    for s in range(8):
        high, low = split(dense_ref[s])
        v_high, v_low = split(v_rows(s))
        y.append(dot(v_high, high) + dot(v_high, low) + dot(v_low, high))
    for s in range(8):
        source_real, source_imag = y[s][:, :HALF], y[s][:, LANES : LANES + HALF]
        if s == 0:
            real, imag = source_real, source_imag
        else:
            couple_real = SCREEN * y[s][:, HALF:LANES]
            couple_imag = SCREEN * y[s][:, LANES + HALF :]
            matrix = jnp.concatenate(
                [
                    jnp.concatenate([couple_real, -couple_imag], axis=1),
                    jnp.concatenate([couple_imag, couple_real], axis=1),
                ],
                axis=0,
            )
            m_high, m_low = split(matrix)
            x_high, x_low = split(jnp.concatenate([real, imag], axis=0))
            product = dot(m_high, x_high) + dot(m_high, x_low) + dot(m_low, x_high)
            real = product[:HALF] + source_real
            imag = product[HALF:] + source_imag
        out_ref[s, 0] = jnp.concatenate([real[:32], real[32:]], axis=1)
        out_ref[s, 1] = jnp.concatenate([imag[:32], imag[32:]], axis=1)


def tables(count):
    half = np.arange(count) + 0.5
    angle = np.outer(half, half) * (math.pi / count)
    table = np.concatenate([np.cos(angle), np.sin(angle)]).astype(np.float32)
    high = table.astype(jnp.bfloat16)
    low = (table - high.astype(np.float32)).astype(jnp.bfloat16)
    return np.concatenate([high, low]).reshape(4, count, count)


def vmem(n):
    return [pl.BlockSpec(memory_space=pltpu.VMEM)] * n


def pack(lesser, greater, v_blocks, slots):
    return pl.pallas_call(
        pack_kernel,
        out_shape=(
            pltpu.VMEM((64, 16, LANES), F32),
            pltpu.VMEM((8, LANES), F32),
            pltpu.VMEM((4, 512, 512), BF16),
        ),
        in_specs=vmem(4) + [pl.BlockSpec(memory_space=pl.ANY)],
        out_specs=tuple(vmem(3)),
        scratch_shapes=[pltpu.SemaphoreType.DMA],
        name="pack",
    )(
        lesser.reshape(512, LANES),
        greater.reshape(512, LANES),
        v_blocks,
        slots.reshape(32, LANES),
        jnp.asarray(tables(512)),
    )


def correlate(data, side, table):
    return pl.pallas_call(
        correlate_kernel,
        out_shape=jax.ShapeDtypeStruct((1024, LANES), F32),
        in_specs=vmem(3),
        out_specs=vmem(1)[0],
        compiler_params=pltpu.CompilerParams(vmem_limit_bytes=40 << 20),
        name="correlate",
    )(data.reshape(64, 2, 8, LANES), side, table)


def screen(data):
    return pl.pallas_call(
        screen_kernel,
        out_shape=jax.ShapeDtypeStruct((8, 2, 32, LANES), F32),
        in_specs=vmem(1),
        out_specs=vmem(1)[0],
        scratch_shapes=[
            pltpu.VMEM((4, 32, LANES), F32),
            pltpu.VMEM((2, 32, LANES), F32),
            pltpu.VMEM((8, HALF, 256), F32),
        ],
        compiler_params=pltpu.CompilerParams(vmem_limit_bytes=40 << 20),
        name="screen",
    )(data)


def shards(g_lesser, g_greater, v_blocks, slots):
    data, side, table = pack(g_lesser, g_greater, v_blocks, slots)
    data = lax.all_to_all(data, "energy", 0, 0, tiled=True)
    data = correlate(data, side, table).reshape(512, 1, 256)
    data = lax.all_to_all(data, ("energy", "cuts"), 0, 0, tiled=True)
    blocks = screen(data.reshape(1024, LANES)).reshape(8, 64, LANES)
    blocks = lax.all_to_all(blocks, "cuts", 0, 0, tiled=True)
    return blocks.reshape(8, 2, 4096).transpose(1, 0, 2).reshape(2, 8, 1, 4096)


def solution(mesh):
    placed = (
        P(None, "energy", "cuts", None),
        P(None, "energy", "cuts", None),
        P("cuts", None, None),
        P("cuts", None),
    )
    return jax.shard_map(
        shards,
        mesh=mesh,
        in_specs=placed,
        out_specs=P(None, "energy", "cuts", None),
        check_vma=False,
    )
```

```python
import functools
import math

import jax
import jax.numpy as jnp
import numpy as np
from jax import lax
from jax.experimental import pallas as pl
from jax.experimental.pallas import tpu as pltpu
from jax.sharding import PartitionSpec as P

SCREEN = 0.08
F32 = jnp.float32
BF16 = jnp.bfloat16
LANES = 128
HALF = 64


def split(x):
    high = x.astype(BF16)
    return high, (x - high.astype(F32)).astype(BF16)


def left_half(shape):
    return lax.broadcasted_iota(jnp.int32, shape, len(shape) - 1) < HALF


def dot(a, b):
    return jnp.dot(a, b, preferred_element_type=F32)


def pack_kernel(
    lesser_ref, greater_ref, v_ref, slots_ref, table_hbm, out_ref, side_ref, table_ref, sem
):
    copy = pltpu.make_async_copy(table_hbm, table_ref, sem)
    copy.start()
    me = lax.axis_index("energy")
    slot = slots_ref[pl.ds(me // 2, 1), :].astype(F32)
    slot = jnp.where(me % 2 == 0, slot, pltpu.roll(slot, HALF, 1))[:, :HALF]
    side = jnp.concatenate([slot, v_ref[0, pl.ds(me, 1), :]], axis=1)
    side_ref[...] = jnp.broadcast_to(side, (8, LANES))
    left = left_half((8, LANES))
    for tile in range(32):
        for which, ref in enumerate((lesser_ref, greater_ref)):
            real = ref[pl.ds(tile, 8, stride=32), :]
            imag = ref[pl.ds(256 + tile, 8, stride=32), :]
            rows = pl.ds(which * 8, 8)
            out_ref[2 * tile, rows, :] = jnp.where(left, real, pltpu.roll(imag, HALF, 1))
            out_ref[2 * tile + 1, rows, :] = jnp.where(left, pltpu.roll(real, HALF, 1), imag)
    copy.wait()


def correlate_kernel(data_ref, side_ref, table_ref, out_ref):
    count = 512
    left = left_half((count, LANES))
    sign = jnp.where(left, 1.0, -1.0).astype(F32)

    def turned(x):
        return pltpu.roll(x, HALF, 1)

    out_ref[pl.ds(1, count, stride=2), :] = jnp.broadcast_to(side_ref[pl.ds(0, 1), :], (count, LANES))

    lesser = data_ref[:, 0].reshape(count, LANES)
    greater = data_ref[:, 1].reshape(count, LANES)
    sig_high, sig_low = split(jnp.concatenate([lesser, greater], axis=1))
    both = jnp.concatenate([sig_high, sig_low], axis=1)
    cosines = dot(table_ref[0], both)
    sines = dot(table_ref[1], both)
    cosines = cosines[:, :256] + cosines[:, 256:] + dot(table_ref[2], sig_high)
    sines = sines[:, :256] + sines[:, 256:] + dot(table_ref[3], sig_high)
    cos_a, cos_b = cosines[:, :LANES], cosines[:, LANES:]
    sin_a, sin_b = sines[:, :LANES], sines[:, LANES:]
    shift_a, shift_b = sign * turned(sin_a), sign * turned(sin_b)

    def times_conjugate(a, b):
        other_b = turned(b)
        real_b = jnp.where(left, b, other_b)
        imag_b = jnp.where(left, other_b, b)
        return a * real_b + (sign * turned(a)) * imag_b

    plus = times_conjugate(cos_a + shift_a, cos_b + shift_b)
    minus = times_conjugate(cos_a - shift_a, cos_b - shift_b)
    for_cos = -sign * turned(plus + minus)
    for_sin = minus - plus
    scale = 1.0 / (2 * count * math.sqrt(count))

    def turn(i):
        column = table_ref[i, :, :LANES][:, :1].astype(F32)
        column += table_ref[i + 2, :, :LANES][:, :1].astype(F32)
        return jnp.broadcast_to(column * scale, (count, LANES))

    turn_cos, turn_sin = turn(0), turn(1)
    cos_high, cos_low = split(turn_cos * for_cos - turn_sin * for_sin)
    sin_high, sin_low = split(turn_sin * for_cos + turn_cos * for_sin)
    result = dot(table_ref[0], jnp.concatenate([cos_high, cos_low], axis=1))
    result += dot(table_ref[1], jnp.concatenate([sin_high, sin_low], axis=1))
    result = result[:, :LANES] + result[:, LANES:]
    result += dot(table_ref[2], cos_high) + dot(table_ref[3], sin_high)
    out_ref[pl.ds(0, count, stride=2), :] = result


def repeated_row(ref, row, times):
    tile = jnp.broadcast_to(ref[pl.ds(row, 1), :], (16, LANES)).astype(BF16)
    return jnp.concatenate([tile] * times, axis=0)


def screen_kernel(data_ref, out_ref, parts_ref, lines_ref, dense_ref):
    left32 = left_half((32, LANES))
    row_iota = lax.broadcasted_iota(jnp.int32, (HALF, LANES), 0).astype(F32).astype(BF16)
    column_iota = lax.broadcasted_iota(jnp.int32, (LANES, LANES), 0).astype(F32).astype(BF16)
    wide_iota = lax.broadcasted_iota(jnp.int32, (LANES, 256), 1).astype(F32).astype(BF16)
    zero = jnp.zeros((), BF16)
    one = jnp.ones((), BF16)

    def lines(s, side):
        return [data_ref[pl.ds(2 * s + side + 16 * odd, 32, stride=32), :] for odd in range(2)]

    def join(even, odd):
        return jnp.where(left32, even, pltpu.roll(odd, HALF, 1))

    def join_right(even, odd):
        return jnp.where(left32, pltpu.roll(even, HALF, 1), odd)

    def v_rows(s):
        return jnp.concatenate(lines(s, 1), axis=0)[:, HALF:]

    def scatter(s, parts_ref, lines_ref):
        polar = lines(s, 0)
        for i, part in enumerate((*split(join(*polar)), *split(join_right(*polar)))):
            parts_ref[i] = part.astype(F32)
        slot = join(*lines(s, 1)).astype(jnp.int32)
        column = slot & 127
        moved = HALF + (column & 1) * 32 + ((column - HALF) >> 1)
        lines_ref[0] = (slot >> 7).astype(F32)
        column = jnp.where(column < HALF, column, moved)
        lines_ref[1] = column.astype(F32)
        lines_ref[2] = ((slot >> 7) & 31).astype(F32)
        places = (column + ((slot >> 12) << 7)).astype(F32).T.astype(BF16)

        def tall(r):
            hit = repeated_row(lines_ref.at[0], r, 4) == row_iota
            first = [jnp.where(hit, repeated_row(parts_ref.at[i], r, 4), zero) for i in range(4)]
            place = repeated_row(lines_ref.at[1], r, 8) == column_iota
            return jnp.concatenate(first, axis=0), jnp.where(place, one, zero)

        def wide(r):
            hit = repeated_row(lines_ref.at[2], r, 2) == row_iota[:32]
            first = [jnp.where(hit, repeated_row(parts_ref.at[i], r, 2), zero) for i in range(4)]
            place = jnp.broadcast_to(places[:, r : r + 1], (LANES, 256)) == wide_iota
            return jnp.concatenate(first, axis=0), jnp.where(place, one, zero)

        dense = None
        other = None
        for r in range(0, 32, 2):
            if r % 4 == 2:
                pairs = [wide(r), wide(r + 1)]
                first = jnp.concatenate([pair[0] for pair in pairs], axis=1)
                term = dot(first, jnp.concatenate([pair[1] for pair in pairs], axis=0))
                other = term if other is None else other + term
            else:
                pairs = [tall(r), tall(r + 1)]
                first = jnp.concatenate([pair[0] for pair in pairs], axis=1)
                second = jnp.concatenate([pair[1] for pair in pairs], axis=1)
                term = lax.dot_general(
                    first, second, (((1,), (1,)), ((), ())), preferred_element_type=F32
                )
                dense = term if dense is None else dense + term
        real = dense[0:64] + dense[64:128]
        imag = dense[128:192] + dense[192:256]
        other_real = other[0:32] + other[32:64]
        other_imag = other[64:96] + other[96:128]
        real += jnp.concatenate([other_real[:, :LANES], other_real[:, LANES:]], axis=0)
        imag += jnp.concatenate([other_imag[:, :LANES], other_imag[:, LANES:]], axis=0)
        dense_ref[s] = jnp.concatenate([real, imag], axis=1)

    for s in range(8):
        scatter(s, parts_ref.at[s], lines_ref.at[s])

    y = []
    for s in range(8):
        high, low = split(dense_ref[s])
        v_high, v_low = split(v_rows(s))
        y.append(dot(v_high, high) + dot(v_high, low) + dot(v_low, high))
    for s in range(8):
        source_real, source_imag = y[s][:, :HALF], y[s][:, LANES : LANES + HALF]
        if s == 0:
            real, imag = source_real, source_imag
        else:
            couple_real = SCREEN * y[s][:, HALF:LANES]
            couple_imag = SCREEN * y[s][:, LANES + HALF :]
            matrix = jnp.concatenate(
                [
                    jnp.concatenate([couple_real, -couple_imag], axis=1),
                    jnp.concatenate([couple_imag, couple_real], axis=1),
                ],
                axis=0,
            )
            m_high, m_low = split(matrix)
            x_high, x_low = split(jnp.concatenate([real, imag], axis=0))
            product = dot(m_high, x_high) + dot(m_high, x_low) + dot(m_low, x_high)
            real = product[:HALF] + source_real
            imag = product[HALF:] + source_imag
        out_ref[s, 0] = jnp.concatenate([real[:32], real[32:]], axis=1)
        out_ref[s, 1] = jnp.concatenate([imag[:32], imag[32:]], axis=1)


def tables(count):
    half = np.arange(count) + 0.5
    angle = np.outer(half, half) * (math.pi / count)
    table = np.concatenate([np.cos(angle), np.sin(angle)]).astype(np.float32)
    high = table.astype(jnp.bfloat16)
    low = (table - high.astype(np.float32)).astype(jnp.bfloat16)
    return np.concatenate([high, low]).reshape(4, count, count)


def vmem(n):
    return [pl.BlockSpec(memory_space=pltpu.VMEM)] * n


def pack(lesser, greater, v_blocks, slots):
    return pl.pallas_call(
        pack_kernel,
        out_shape=(
            pltpu.VMEM((64, 16, LANES), F32),
            pltpu.VMEM((8, LANES), F32),
            pltpu.VMEM((4, 512, 512), BF16),
        ),
        in_specs=vmem(4) + [pl.BlockSpec(memory_space=pl.ANY)],
        out_specs=tuple(vmem(3)),
        scratch_shapes=[pltpu.SemaphoreType.DMA],
        name="pack",
    )(
        lesser.reshape(512, LANES),
        greater.reshape(512, LANES),
        v_blocks,
        slots.reshape(32, LANES),
        jnp.asarray(tables(512)),
    )


def correlate(data, side, table):
    return pl.pallas_call(
        correlate_kernel,
        out_shape=jax.ShapeDtypeStruct((1024, LANES), F32),
        in_specs=vmem(3),
        out_specs=vmem(1)[0],
        compiler_params=pltpu.CompilerParams(vmem_limit_bytes=40 << 20),
        name="correlate",
    )(data.reshape(64, 2, 8, LANES), side, table)


def screen(data):
    return pl.pallas_call(
        screen_kernel,
        out_shape=jax.ShapeDtypeStruct((8, 2, 32, LANES), F32),
        in_specs=vmem(1),
        out_specs=vmem(1)[0],
        scratch_shapes=[
            pltpu.VMEM((8, 4, 32, LANES), F32),
            pltpu.VMEM((8, 3, 32, LANES), F32),
            pltpu.VMEM((8, HALF, 256), F32),
        ],
        compiler_params=pltpu.CompilerParams(vmem_limit_bytes=40 << 20),
        name="screen",
    )(data)


def shards(g_lesser, g_greater, v_blocks, slots):
    data, side, table = pack(g_lesser, g_greater, v_blocks, slots)
    data = lax.all_to_all(data, "energy", 0, 0, tiled=True)
    data = correlate(data, side, table).reshape(512, 1, 256)
    data = lax.all_to_all(data, ("energy", "cuts"), 0, 0, tiled=True)
    blocks = screen(data.reshape(1024, LANES)).reshape(8, 64, LANES)
    blocks = lax.all_to_all(blocks, "cuts", 0, 0, tiled=True)
    return blocks.reshape(8, 2, 4096).transpose(1, 0, 2).reshape(2, 8, 1, 4096)


def solution(mesh):
    placed = (
        P(None, "energy", "cuts", None),
        P(None, "energy", "cuts", None),
        P("cuts", None, None),
        P("cuts", None),
    )
    return jax.shard_map(
        shards,
        mesh=mesh,
        in_specs=placed,
        out_specs=P(None, "energy", "cuts", None),
        check_vma=False,
    )
```

```python
import functools
import math

import jax
import jax.numpy as jnp
import numpy as np
from jax import lax
from jax.experimental import pallas as pl
from jax.experimental.pallas import tpu as pltpu
from jax.sharding import PartitionSpec as P

SCREEN = 0.08
F32 = jnp.float32
BF16 = jnp.bfloat16
LANES = 128
HALF = 64


def split(x):
    high = x.astype(BF16)
    return high, (x - high.astype(F32)).astype(BF16)


def left_half(shape):
    return lax.broadcasted_iota(jnp.int32, shape, len(shape) - 1) < HALF


def dot(a, b):
    return jnp.dot(a, b, preferred_element_type=F32)


def pack_kernel(
    lesser_hbm, greater_hbm, table_hbm, v_hbm, slots_hbm, out_ref, side_ref, table_ref,
    lesser_ref, greater_ref, v_ref, slots_ref, sems,
):
    copies = [
        pltpu.make_async_copy(lesser_hbm, lesser_ref, sems.at[0]),
        pltpu.make_async_copy(greater_hbm, greater_ref, sems.at[1]),
    ]
    for i in range(4):
        copies.append(pltpu.make_async_copy(table_hbm.at[i], table_ref.at[i], sems.at[2 + i]))
    copies.append(pltpu.make_async_copy(v_hbm, v_ref, sems.at[6]))
    copies.append(pltpu.make_async_copy(slots_hbm, slots_ref, sems.at[7]))
    for copy in copies:
        copy.start()
    left = left_half((8, LANES))
    for which, ref in enumerate((lesser_ref, greater_ref)):
        copies[which].wait()
        for tile in range(32):
            real = ref[pl.ds(tile, 8, stride=32), :]
            imag = ref[pl.ds(256 + tile, 8, stride=32), :]
            rows = pl.ds(which * 8, 8)
            out_ref[2 * tile, rows, :] = jnp.where(left, real, pltpu.roll(imag, HALF, 1))
            out_ref[2 * tile + 1, rows, :] = jnp.where(left, pltpu.roll(real, HALF, 1), imag)
    for copy in copies[2:]:
        copy.wait()
    me = lax.axis_index("energy")
    slot = slots_ref[pl.ds(me // 2, 1), :].astype(F32)
    slot = jnp.where(me % 2 == 0, slot, pltpu.roll(slot, HALF, 1))[:, :HALF]
    side = jnp.concatenate([slot, v_ref[0, pl.ds(me, 1), :]], axis=1)
    side_ref[...] = jnp.broadcast_to(side, (8, LANES))


def correlate_kernel(data_ref, side_ref, table_ref, out_ref):
    count = 512
    left = left_half((count, LANES))
    sign = jnp.where(left, 1.0, -1.0).astype(F32)

    def turned(x):
        return pltpu.roll(x, HALF, 1)

    out_ref[pl.ds(1, count, stride=2), :] = jnp.broadcast_to(side_ref[pl.ds(0, 1), :], (count, LANES))

    lesser = data_ref[:, 0].reshape(count, LANES)
    greater = data_ref[:, 1].reshape(count, LANES)
    sig_high, sig_low = split(jnp.concatenate([lesser, greater], axis=1))
    both = jnp.concatenate([sig_high, sig_low], axis=1)
    cosines = dot(table_ref[0], both)
    sines = dot(table_ref[1], both)
    cosines = cosines[:, :256] + cosines[:, 256:] + dot(table_ref[2], sig_high)
    sines = sines[:, :256] + sines[:, 256:] + dot(table_ref[3], sig_high)
    cos_a, cos_b = cosines[:, :LANES], cosines[:, LANES:]
    sin_a, sin_b = sines[:, :LANES], sines[:, LANES:]
    shift_a, shift_b = sign * turned(sin_a), sign * turned(sin_b)

    def times_conjugate(a, b):
        other_b = turned(b)
        real_b = jnp.where(left, b, other_b)
        imag_b = jnp.where(left, other_b, b)
        return a * real_b + (sign * turned(a)) * imag_b

    plus = times_conjugate(cos_a + shift_a, cos_b + shift_b)
    minus = times_conjugate(cos_a - shift_a, cos_b - shift_b)
    for_cos = -sign * turned(plus + minus)
    for_sin = minus - plus
    scale = 1.0 / (2 * count * math.sqrt(count))

    def turn(i):
        column = table_ref[i, :, :LANES][:, :1].astype(F32)
        column += table_ref[i + 2, :, :LANES][:, :1].astype(F32)
        return jnp.broadcast_to(column * scale, (count, LANES))

    turn_cos, turn_sin = turn(0), turn(1)
    cos_high, cos_low = split(turn_cos * for_cos - turn_sin * for_sin)
    sin_high, sin_low = split(turn_sin * for_cos + turn_cos * for_sin)
    result = dot(table_ref[0], jnp.concatenate([cos_high, cos_low], axis=1))
    result += dot(table_ref[1], jnp.concatenate([sin_high, sin_low], axis=1))
    result = result[:, :LANES] + result[:, LANES:]
    result += dot(table_ref[2], cos_high) + dot(table_ref[3], sin_high)
    out_ref[pl.ds(0, count, stride=2), :] = result


def repeated_row(ref, row, times):
    tile = jnp.broadcast_to(ref[pl.ds(row, 1), :], (16, LANES)).astype(BF16)
    return jnp.concatenate([tile] * times, axis=0)


def screen_kernel(data_ref, out_ref, parts_ref, lines_ref, dense_ref):
    left32 = left_half((32, LANES))
    row_iota = lax.broadcasted_iota(jnp.int32, (HALF, LANES), 0).astype(F32).astype(BF16)
    column_iota = lax.broadcasted_iota(jnp.int32, (LANES, LANES), 0).astype(F32).astype(BF16)
    wide_iota = lax.broadcasted_iota(jnp.int32, (LANES, 256), 1).astype(F32).astype(BF16)
    zero = jnp.zeros((), BF16)
    one = jnp.ones((), BF16)

    def lines(s, side):
        return [data_ref[pl.ds(2 * s + side + 16 * odd, 32, stride=32), :] for odd in range(2)]

    def join(even, odd):
        return jnp.where(left32, even, pltpu.roll(odd, HALF, 1))

    def join_right(even, odd):
        return jnp.where(left32, pltpu.roll(even, HALF, 1), odd)

    def v_rows(s):
        return jnp.concatenate(lines(s, 1), axis=0)[:, HALF:]

    def scatter(s, parts_ref, lines_ref):
        polar = lines(s, 0)
        for i, part in enumerate((*split(join(*polar)), *split(join_right(*polar)))):
            parts_ref[i] = part.astype(F32)
        slot = join(*lines(s, 1)).astype(jnp.int32)
        column = slot & 127
        moved = HALF + (column & 1) * 32 + ((column - HALF) >> 1)
        lines_ref[0] = (slot >> 7).astype(F32)
        column = jnp.where(column < HALF, column, moved)
        lines_ref[1] = column.astype(F32)
        lines_ref[2] = ((slot >> 7) & 31).astype(F32)
        places = (column + ((slot >> 12) << 7)).astype(F32).T.astype(BF16)

        def tall(r):
            hit = repeated_row(lines_ref.at[0], r, 4) == row_iota
            first = [jnp.where(hit, repeated_row(parts_ref.at[i], r, 4), zero) for i in range(4)]
            place = repeated_row(lines_ref.at[1], r, 8) == column_iota
            return jnp.concatenate(first, axis=0), jnp.where(place, one, zero)

        def wide(r):
            hit = repeated_row(lines_ref.at[2], r, 2) == row_iota[:32]
            first = [jnp.where(hit, repeated_row(parts_ref.at[i], r, 2), zero) for i in range(4)]
            place = jnp.broadcast_to(places[:, r : r + 1], (LANES, 256)) == wide_iota
            return jnp.concatenate(first, axis=0), jnp.where(place, one, zero)

        dense = None
        other = None
        for r in range(0, 32, 2):
            if r % 4 == 2:
                pairs = [wide(r), wide(r + 1)]
                first = jnp.concatenate([pair[0] for pair in pairs], axis=1)
                term = dot(first, jnp.concatenate([pair[1] for pair in pairs], axis=0))
                other = term if other is None else other + term
            else:
                pairs = [tall(r), tall(r + 1)]
                first = jnp.concatenate([pair[0] for pair in pairs], axis=1)
                second = jnp.concatenate([pair[1] for pair in pairs], axis=1)
                term = lax.dot_general(
                    first, second, (((1,), (1,)), ((), ())), preferred_element_type=F32
                )
                dense = term if dense is None else dense + term
        real = dense[0:64] + dense[64:128]
        imag = dense[128:192] + dense[192:256]
        other_real = other[0:32] + other[32:64]
        other_imag = other[64:96] + other[96:128]
        real += jnp.concatenate([other_real[:, :LANES], other_real[:, LANES:]], axis=0)
        imag += jnp.concatenate([other_imag[:, :LANES], other_imag[:, LANES:]], axis=0)
        dense_ref[s] = jnp.concatenate([real, imag], axis=1)

    for s in range(8):
        scatter(s, parts_ref.at[s], lines_ref.at[s])

    y = []
    for s in range(8):
        high, low = split(dense_ref[s])
        v_high, v_low = split(v_rows(s))
        y.append(dot(v_high, high) + dot(v_high, low) + dot(v_low, high))
    def times(matrix, x):
        m_high, m_low = split(matrix)
        x_high, x_low = split(x)
        return dot(m_high, x_high) + dot(m_high, x_low) + dot(m_low, x_high)

    steps = []
    for s in range(8):
        source = jnp.concatenate([y[s][:, :HALF], y[s][:, LANES : LANES + HALF]], axis=0)
        couple_real = SCREEN * y[s][:, HALF:LANES]
        couple_imag = SCREEN * y[s][:, LANES + HALF :]
        matrix = jnp.concatenate(
            [
                jnp.concatenate([couple_real, -couple_imag], axis=1),
                jnp.concatenate([couple_imag, couple_real], axis=1),
            ],
            axis=0,
        )
        steps.append((matrix, source))
    x = [steps[0][1]]
    pairs = []
    for s in (1, 3, 5):
        joined = times(steps[s + 1][0], jnp.concatenate(steps[s], axis=1))
        pairs.append((joined[:, :LANES], joined[:, LANES:] + steps[s + 1][1]))
    for i, s in enumerate((1, 3, 5)):
        x.append(times(steps[s][0], x[s - 1]) + steps[s][1])
        x.append(times(pairs[i][0], x[s - 1]) + pairs[i][1])
    x.append(times(steps[7][0], x[6]) + steps[7][1])
    for s in range(8):
        for part in range(2):
            rows = x[s][part * HALF : (part + 1) * HALF]
            out_ref[s, part] = jnp.concatenate([rows[:32], rows[32:]], axis=1)


def tables(count):
    half = np.arange(count) + 0.5
    angle = np.outer(half, half) * (math.pi / count)
    table = np.concatenate([np.cos(angle), np.sin(angle)]).astype(np.float32)
    high = table.astype(jnp.bfloat16)
    low = (table - high.astype(np.float32)).astype(jnp.bfloat16)
    return np.concatenate([high, low]).reshape(4, count, count)


def vmem(n):
    return [pl.BlockSpec(memory_space=pltpu.VMEM)] * n


def pack(lesser, greater, v_blocks, slots):
    return pl.pallas_call(
        pack_kernel,
        out_shape=(
            pltpu.VMEM((64, 16, LANES), F32),
            pltpu.VMEM((8, LANES), F32),
            pltpu.VMEM((4, 512, 512), BF16),
        ),
        in_specs=[pl.BlockSpec(memory_space=pl.ANY)] * 5,
        out_specs=tuple(vmem(3)),
        scratch_shapes=[
            pltpu.VMEM((512, LANES), F32),
            pltpu.VMEM((512, LANES), F32),
            pltpu.VMEM((1, HALF, HALF), F32),
            pltpu.VMEM((32, LANES), jnp.int32),
            pltpu.SemaphoreType.DMA((8,)),
        ],
        name="pack",
    )(
        lesser.reshape(512, LANES),
        greater.reshape(512, LANES),
        jnp.asarray(tables(512)),
        v_blocks,
        slots.reshape(32, LANES),
    )


def correlate(data, side, table):
    return pl.pallas_call(
        correlate_kernel,
        out_shape=jax.ShapeDtypeStruct((1024, LANES), F32),
        in_specs=vmem(3),
        out_specs=vmem(1)[0],
        compiler_params=pltpu.CompilerParams(vmem_limit_bytes=40 << 20),
        name="correlate",
    )(data.reshape(64, 2, 8, LANES), side, table)


def screen(data):
    return pl.pallas_call(
        screen_kernel,
        out_shape=jax.ShapeDtypeStruct((8, 2, 32, LANES), F32),
        in_specs=vmem(1),
        out_specs=vmem(1)[0],
        scratch_shapes=[
            pltpu.VMEM((8, 4, 32, LANES), F32),
            pltpu.VMEM((8, 3, 32, LANES), F32),
            pltpu.VMEM((8, HALF, 256), F32),
        ],
        compiler_params=pltpu.CompilerParams(vmem_limit_bytes=40 << 20),
        name="screen",
    )(data)


def shards(g_lesser, g_greater, v_blocks, slots):
    data, side, table = pack(g_lesser, g_greater, v_blocks, slots)
    data = lax.all_to_all(data, "energy", 0, 0, tiled=True)
    data = correlate(data, side, table).reshape(512, 1, 256)
    data = lax.all_to_all(data, ("energy", "cuts"), 0, 0, tiled=True)
    blocks = screen(data.reshape(1024, LANES)).reshape(8, 64, LANES)
    blocks = lax.all_to_all(blocks, "cuts", 0, 0, tiled=True)
    return blocks.reshape(8, 2, 4096).transpose(1, 0, 2).reshape(2, 8, 1, 4096)


def solution(mesh):
    placed = (
        P(None, "energy", "cuts", None),
        P(None, "energy", "cuts", None),
        P("cuts", None, None),
        P("cuts", None),
    )
    return jax.shard_map(
        shards,
        mesh=mesh,
        in_specs=placed,
        out_specs=P(None, "energy", "cuts", None),
        check_vma=False,
    )
```

```python
import functools
import math

import jax
import jax.numpy as jnp
import numpy as np
from jax import lax
from jax.experimental import pallas as pl
from jax.experimental.pallas import tpu as pltpu
from jax.sharding import PartitionSpec as P

SCREEN = 0.08
F32 = jnp.float32
BF16 = jnp.bfloat16
LANES = 128
HALF = 64


def split(x):
    high = x.astype(BF16)
    return high, (x - high.astype(F32)).astype(BF16)


def left_half(shape):
    return lax.broadcasted_iota(jnp.int32, shape, len(shape) - 1) < HALF


def dot(a, b):
    return jnp.dot(a, b, preferred_element_type=F32)


def pack_kernel(
    lesser_hbm, greater_hbm, table_hbm, v_hbm, slots_hbm, out_ref, side_ref, table_ref,
    lesser_ref, greater_ref, v_ref, slots_ref, sems,
):
    copies = [
        pltpu.make_async_copy(lesser_hbm, lesser_ref, sems.at[0]),
        pltpu.make_async_copy(greater_hbm, greater_ref, sems.at[1]),
    ]
    for i in range(4):
        copies.append(pltpu.make_async_copy(table_hbm.at[i], table_ref.at[i], sems.at[2 + i]))
    copies.append(pltpu.make_async_copy(v_hbm, v_ref, sems.at[6]))
    copies.append(pltpu.make_async_copy(slots_hbm, slots_ref, sems.at[7]))
    for copy in copies:
        copy.start()
    left = left_half((8, LANES))
    for which, ref in enumerate((lesser_ref, greater_ref)):
        copies[which].wait()
        for tile in range(32):
            real = ref[pl.ds(tile, 8, stride=32), :]
            imag = ref[pl.ds(256 + tile, 8, stride=32), :]
            rows = pl.ds(which * 8, 8)
            out_ref[2 * tile, rows, :] = jnp.where(left, real, pltpu.roll(imag, HALF, 1))
            out_ref[2 * tile + 1, rows, :] = jnp.where(left, pltpu.roll(real, HALF, 1), imag)
    for copy in copies[2:]:
        copy.wait()
    me = lax.axis_index("energy")
    slot = slots_ref[pl.ds(me // 2, 1), :].astype(F32)
    slot = jnp.where(me % 2 == 0, slot, pltpu.roll(slot, HALF, 1))[:, :HALF]
    side = jnp.concatenate([slot, v_ref[0, pl.ds(me, 1), :]], axis=1)
    side_ref[...] = jnp.broadcast_to(side, (8, LANES))


def correlate_kernel(data_ref, side_ref, table_ref, out_ref):
    count = 512
    left = left_half((count, LANES))
    sign = jnp.where(left, 1.0, -1.0).astype(F32)

    def turned(x):
        return pltpu.roll(x, HALF, 1)

    out_ref[pl.ds(1, count, stride=2), :] = jnp.broadcast_to(side_ref[pl.ds(0, 1), :], (count, LANES))

    lesser = data_ref[:, 0].reshape(count, LANES)
    greater = data_ref[:, 1].reshape(count, LANES)
    sig_high, sig_low = split(jnp.concatenate([lesser, greater], axis=1))
    both = jnp.concatenate([sig_high, sig_low], axis=1)
    cosines = dot(table_ref[0], both)
    sines = dot(table_ref[1], both)
    cosines = cosines[:, :256] + cosines[:, 256:] + dot(table_ref[2], sig_high)
    sines = sines[:, :256] + sines[:, 256:] + dot(table_ref[3], sig_high)
    cos_a, cos_b = cosines[:, :LANES], cosines[:, LANES:]
    sin_a, sin_b = sines[:, :LANES], sines[:, LANES:]
    shift_a, shift_b = sign * turned(sin_a), sign * turned(sin_b)

    def times_conjugate(a, b):
        other_b = turned(b)
        real_b = jnp.where(left, b, other_b)
        imag_b = jnp.where(left, other_b, b)
        return a * real_b + (sign * turned(a)) * imag_b

    plus = times_conjugate(cos_a + shift_a, cos_b + shift_b)
    minus = times_conjugate(cos_a - shift_a, cos_b - shift_b)
    for_cos = -sign * turned(plus + minus)
    for_sin = minus - plus
    scale = 1.0 / (2 * count * math.sqrt(count))

    def turn(i):
        column = table_ref[i, :, :LANES][:, :1].astype(F32)
        column += table_ref[i + 2, :, :LANES][:, :1].astype(F32)
        return jnp.broadcast_to(column * scale, (count, LANES))

    turn_cos, turn_sin = turn(0), turn(1)
    cos_high, cos_low = split(turn_cos * for_cos - turn_sin * for_sin)
    sin_high, sin_low = split(turn_sin * for_cos + turn_cos * for_sin)
    result = dot(table_ref[0], jnp.concatenate([cos_high, cos_low], axis=1))
    result += dot(table_ref[1], jnp.concatenate([sin_high, sin_low], axis=1))
    result = result[:, :LANES] + result[:, LANES:]
    result += dot(table_ref[2], cos_high) + dot(table_ref[3], sin_high)
    out_ref[pl.ds(0, count, stride=2), :] = result


def repeated_row(ref, row, times):
    tile = jnp.broadcast_to(ref[pl.ds(row, 1), :], (16, LANES)).astype(BF16)
    return jnp.concatenate([tile] * times, axis=0)


def screen_kernel(data_ref, out_ref, parts_ref, lines_ref, dense_ref):
    left32 = left_half((32, LANES))
    row_iota = lax.broadcasted_iota(jnp.int32, (HALF, LANES), 0).astype(F32).astype(BF16)
    column_iota = lax.broadcasted_iota(jnp.int32, (LANES, LANES), 0).astype(F32).astype(BF16)
    wide_iota = lax.broadcasted_iota(jnp.int32, (LANES, 256), 1).astype(F32).astype(BF16)
    zero = jnp.zeros((), BF16)
    one = jnp.ones((), BF16)

    def lines(s, side):
        return [data_ref[pl.ds(2 * s + side + 16 * odd, 32, stride=32), :] for odd in range(2)]

    def join(even, odd):
        return jnp.where(left32, even, pltpu.roll(odd, HALF, 1))

    def join_right(even, odd):
        return jnp.where(left32, pltpu.roll(even, HALF, 1), odd)

    def v_rows(s):
        return jnp.concatenate(lines(s, 1), axis=0)[:, HALF:]

    def scatter(s, parts_ref, lines_ref):
        polar = lines(s, 0)
        for i, part in enumerate((*split(join(*polar)), *split(join_right(*polar)))):
            parts_ref[i] = part.astype(F32)
        slot = join(*lines(s, 1)).astype(jnp.int32)
        column = slot & 127
        moved = HALF + (column & 1) * 32 + ((column - HALF) >> 1)
        lines_ref[0] = (slot >> 7).astype(F32)
        column = jnp.where(column < HALF, column, moved)
        lines_ref[1] = column.astype(F32)
        lines_ref[2] = ((slot >> 7) & 31).astype(F32)
        places = (column + ((slot >> 12) << 7)).astype(F32).T.astype(BF16)

        def tall(r):
            hit = repeated_row(lines_ref.at[0], r, 4) == row_iota
            first = [jnp.where(hit, repeated_row(parts_ref.at[i], r, 4), zero) for i in range(4)]
            place = repeated_row(lines_ref.at[1], r, 8) == column_iota
            return jnp.concatenate(first, axis=0), jnp.where(place, one, zero)

        def wide(r):
            hit = repeated_row(lines_ref.at[2], r, 2) == row_iota[:32]
            first = [jnp.where(hit, repeated_row(parts_ref.at[i], r, 2), zero) for i in range(4)]
            place = jnp.broadcast_to(places[:, r : r + 1], (LANES, 256)) == wide_iota
            return jnp.concatenate(first, axis=0), jnp.where(place, one, zero)

        dense = None
        other = None
        for r in range(0, 32, 2):
            if r % 4 == 2:
                pairs = [wide(r), wide(r + 1)]
                first = jnp.concatenate([pair[0] for pair in pairs], axis=1)
                term = dot(first, jnp.concatenate([pair[1] for pair in pairs], axis=0))
                other = term if other is None else other + term
            else:
                pairs = [tall(r), tall(r + 1)]
                first = jnp.concatenate([pair[0] for pair in pairs], axis=1)
                second = jnp.concatenate([pair[1] for pair in pairs], axis=1)
                term = lax.dot_general(
                    first, second, (((1,), (1,)), ((), ())), preferred_element_type=F32
                )
                dense = term if dense is None else dense + term
        real = dense[0:64] + dense[64:128]
        imag = dense[128:192] + dense[192:256]
        other_real = other[0:32] + other[32:64]
        other_imag = other[64:96] + other[96:128]
        real += jnp.concatenate([other_real[:, :LANES], other_real[:, LANES:]], axis=0)
        imag += jnp.concatenate([other_imag[:, :LANES], other_imag[:, LANES:]], axis=0)
        dense_ref[s] = jnp.concatenate([real, imag], axis=1)

    for s in range(8):
        scatter(s, parts_ref.at[s], lines_ref.at[s])

    y = []
    for s in range(8):
        high, low = split(dense_ref[s])
        v_high, v_low = split(v_rows(s))
        y.append(dot(v_high, high) + dot(v_high, low) + dot(v_low, high))
    def times(matrix, x):
        m_high, m_low = split(matrix)
        x_high, x_low = split(x)
        return dot(m_high, x_high) + dot(m_high, x_low) + dot(m_low, x_high)

    steps = []
    for s in range(8):
        source = jnp.concatenate([y[s][:, :HALF], y[s][:, LANES : LANES + HALF]], axis=0)
        couple_real = SCREEN * y[s][:, HALF:LANES]
        couple_imag = SCREEN * y[s][:, LANES + HALF :]
        matrix = jnp.concatenate(
            [
                jnp.concatenate([couple_real, -couple_imag], axis=1),
                jnp.concatenate([couple_imag, couple_real], axis=1),
            ],
            axis=0,
        )
        steps.append((matrix, source))
    x = [steps[0][1]]
    pairs = []
    for s in (1, 3, 5):
        joined = times(steps[s + 1][0], jnp.concatenate(steps[s], axis=1))
        pairs.append((joined[:, :LANES], joined[:, LANES:] + steps[s + 1][1]))
    for i, s in enumerate((1, 3, 5)):
        x.append(times(steps[s][0], x[s - 1]) + steps[s][1])
        x.append(times(pairs[i][0], x[s - 1]) + pairs[i][1])
    x.append(times(steps[7][0], x[6]) + steps[7][1])
    for s in range(8):
        for part in range(2):
            rows = x[s][part * HALF : (part + 1) * HALF]
            out_ref[s, part] = jnp.concatenate([rows[:32], rows[32:]], axis=1)


def tables(count):
    half = np.arange(count) + 0.5
    angle = np.outer(half, half) * (math.pi / count)
    table = np.concatenate([np.cos(angle), np.sin(angle)]).astype(np.float32)
    high = table.astype(jnp.bfloat16)
    low = (table - high.astype(np.float32)).astype(jnp.bfloat16)
    return np.concatenate([high, low]).reshape(4, count, count)


def vmem(n):
    return [pl.BlockSpec(memory_space=pltpu.VMEM)] * n


def pack(lesser, greater, v_blocks, slots):
    return pl.pallas_call(
        pack_kernel,
        out_shape=(
            pltpu.VMEM((64, 16, LANES), F32),
            pltpu.VMEM((8, LANES), F32),
            pltpu.VMEM((4, 512, 512), BF16),
        ),
        in_specs=[pl.BlockSpec(memory_space=pl.ANY)] * 5,
        out_specs=tuple(vmem(3)),
        scratch_shapes=[
            pltpu.VMEM((512, LANES), F32),
            pltpu.VMEM((512, LANES), F32),
            pltpu.VMEM((1, HALF, HALF), F32),
            pltpu.VMEM((32, LANES), jnp.int32),
            pltpu.SemaphoreType.DMA((8,)),
        ],
        name="pack",
    )(
        lesser.reshape(512, LANES),
        greater.reshape(512, LANES),
        jnp.asarray(tables(512)),
        v_blocks,
        slots.reshape(32, LANES),
    )


def correlate(data, side, table):
    return pl.pallas_call(
        correlate_kernel,
        out_shape=jax.ShapeDtypeStruct((1024, LANES), F32),
        in_specs=vmem(3),
        out_specs=vmem(1)[0],
        compiler_params=pltpu.CompilerParams(vmem_limit_bytes=40 << 20),
        name="correlate",
    )(data.reshape(64, 2, 8, LANES), side, table)


def screen(data):
    return pl.pallas_call(
        screen_kernel,
        out_shape=jax.ShapeDtypeStruct((8, 2, 32, LANES), F32),
        in_specs=vmem(1),
        out_specs=vmem(1)[0],
        scratch_shapes=[
            pltpu.VMEM((8, 4, 32, LANES), F32),
            pltpu.VMEM((8, 3, 32, LANES), F32),
            pltpu.VMEM((8, HALF, 256), F32),
        ],
        compiler_params=pltpu.CompilerParams(vmem_limit_bytes=40 << 20),
        name="screen",
    )(data)


def shards(g_lesser, g_greater, v_blocks, slots):
    data, side, table = pack(g_lesser, g_greater, v_blocks, slots)
    data = lax.all_to_all(data.reshape(64, 1, 2048), "energy", 0, 0, tiled=True)
    data = correlate(data, side, table).reshape(512, 1, 256)
    data = lax.all_to_all(data, ("energy", "cuts"), 0, 0, tiled=True)
    blocks = screen(data.reshape(1024, LANES)).reshape(8, 64, LANES)
    blocks = lax.all_to_all(blocks, "cuts", 0, 0, tiled=True)
    return blocks.reshape(8, 2, 4096).transpose(1, 0, 2).reshape(2, 8, 1, 4096)


def solution(mesh):
    placed = (
        P(None, "energy", "cuts", None),
        P(None, "energy", "cuts", None),
        P("cuts", None, None),
        P("cuts", None),
    )
    return jax.shard_map(
        shards,
        mesh=mesh,
        in_specs=placed,
        out_specs=P(None, "energy", "cuts", None),
        check_vma=False,
    )
```

```python
import functools
import math

import jax
import jax.numpy as jnp
import numpy as np
from jax import lax
from jax.experimental import pallas as pl
from jax.experimental.pallas import tpu as pltpu
from jax.sharding import PartitionSpec as P

SCREEN = 0.08
F32 = jnp.float32
BF16 = jnp.bfloat16
LANES = 128
HALF = 64


def split(x):
    high = x.astype(BF16)
    return high, (x - high.astype(F32)).astype(BF16)


def left_half(shape):
    return lax.broadcasted_iota(jnp.int32, shape, len(shape) - 1) < HALF


def dot(a, b):
    return jnp.dot(a, b, preferred_element_type=F32)


def pack_kernel(
    lesser_hbm, greater_hbm, table_hbm, v_hbm, slots_hbm, out_ref, side_ref, table_ref,
    lesser_ref, greater_ref, v_ref, slots_ref, sems,
):
    copies = [
        pltpu.make_async_copy(lesser_hbm, lesser_ref, sems.at[0]),
        pltpu.make_async_copy(greater_hbm, greater_ref, sems.at[1]),
    ]
    for i in range(4):
        copies.append(pltpu.make_async_copy(table_hbm.at[i], table_ref.at[i], sems.at[2 + i]))
    copies.append(pltpu.make_async_copy(v_hbm, v_ref, sems.at[6]))
    copies.append(pltpu.make_async_copy(slots_hbm, slots_ref, sems.at[7]))
    for copy in copies:
        copy.start()
    left = left_half((8, LANES))
    for which, ref in enumerate((lesser_ref, greater_ref)):
        copies[which].wait()
        for tile in range(32):
            real = ref[pl.ds(tile, 8, stride=32), :]
            imag = ref[pl.ds(256 + tile, 8, stride=32), :]
            rows = pl.ds(which * 8, 8)
            out_ref[2 * tile, rows, :] = jnp.where(left, real, pltpu.roll(imag, HALF, 1))
            out_ref[2 * tile + 1, rows, :] = jnp.where(left, pltpu.roll(real, HALF, 1), imag)
    for copy in copies[2:]:
        copy.wait()
    me = lax.axis_index("energy")
    slot = slots_ref[pl.ds(me // 2, 1), :].astype(F32)
    slot = jnp.where(me % 2 == 0, slot, pltpu.roll(slot, HALF, 1))[:, :HALF]
    side = jnp.concatenate([slot, v_ref[0, pl.ds(me, 1), :]], axis=1)
    side_ref[...] = jnp.broadcast_to(side, (8, LANES))


def correlate_kernel(data_ref, side_ref, table_ref, out_ref):
    count = 512
    left = left_half((count, LANES))
    sign = jnp.where(left, 1.0, -1.0).astype(F32)

    def turned(x):
        return pltpu.roll(x, HALF, 1)

    out_ref[pl.ds(1, count, stride=2), :] = jnp.broadcast_to(side_ref[pl.ds(0, 1), :], (count, LANES))

    lesser = data_ref[:, 0].reshape(count, LANES)
    greater = data_ref[:, 1].reshape(count, LANES)
    sig_high, sig_low = split(jnp.concatenate([lesser, greater], axis=1))
    both = jnp.concatenate([sig_high, sig_low], axis=1)
    cosines = dot(table_ref[0], both)
    sines = dot(table_ref[1], both)
    cosines = cosines[:, :256] + cosines[:, 256:] + dot(table_ref[2], sig_high)
    sines = sines[:, :256] + sines[:, 256:] + dot(table_ref[3], sig_high)
    cos_a, cos_b = cosines[:, :LANES], cosines[:, LANES:]
    sin_a, sin_b = sines[:, :LANES], sines[:, LANES:]
    shift_a, shift_b = sign * turned(sin_a), sign * turned(sin_b)

    def times_conjugate(a, b):
        other_b = turned(b)
        real_b = jnp.where(left, b, other_b)
        imag_b = jnp.where(left, other_b, b)
        return a * real_b + (sign * turned(a)) * imag_b

    plus = times_conjugate(cos_a + shift_a, cos_b + shift_b)
    minus = times_conjugate(cos_a - shift_a, cos_b - shift_b)
    for_cos = -sign * turned(plus + minus)
    for_sin = minus - plus
    scale = 1.0 / (2 * count * math.sqrt(count))

    def turn(i):
        column = table_ref[i, :, :LANES][:, :1].astype(F32)
        column += table_ref[i + 2, :, :LANES][:, :1].astype(F32)
        return jnp.broadcast_to(column * scale, (count, LANES))

    turn_cos, turn_sin = turn(0), turn(1)
    cos_high, cos_low = split(turn_cos * for_cos - turn_sin * for_sin)
    sin_high, sin_low = split(turn_sin * for_cos + turn_cos * for_sin)
    result = dot(table_ref[0], jnp.concatenate([cos_high, cos_low], axis=1))
    result += dot(table_ref[1], jnp.concatenate([sin_high, sin_low], axis=1))
    result = result[:, :LANES] + result[:, LANES:]
    result += dot(table_ref[2], cos_high) + dot(table_ref[3], sin_high)
    out_ref[pl.ds(0, count, stride=2), :] = result


def repeated_row(ref, row, times):
    tile = jnp.broadcast_to(ref[pl.ds(row, 1), :], (16, LANES)).astype(BF16)
    return jnp.concatenate([tile] * times, axis=0)


def screen_kernel(data_ref, out_ref, parts_ref, lines_ref, dense_ref):
    left32 = left_half((32, LANES))
    row_iota = lax.broadcasted_iota(jnp.int32, (HALF, LANES), 0).astype(F32).astype(BF16)
    column_iota = lax.broadcasted_iota(jnp.int32, (LANES, LANES), 0).astype(F32).astype(BF16)
    wide_iota = lax.broadcasted_iota(jnp.int32, (LANES, 256), 1).astype(F32).astype(BF16)
    zero = jnp.zeros((), BF16)
    one = jnp.ones((), BF16)

    def lines(s, side):
        return [data_ref[pl.ds(2 * s + side + 16 * odd, 32, stride=32), :] for odd in range(2)]

    def join(even, odd):
        return jnp.where(left32, even, pltpu.roll(odd, HALF, 1))

    def join_right(even, odd):
        return jnp.where(left32, pltpu.roll(even, HALF, 1), odd)

    def v_rows(s):
        return jnp.concatenate(lines(s, 1), axis=0)[:, HALF:]

    def scatter(s, parts_ref, lines_ref):
        polar = lines(s, 0)
        for i, part in enumerate((*split(join(*polar)), *split(join_right(*polar)))):
            parts_ref[i] = part.astype(F32)
        slot = join(*lines(s, 1)).astype(jnp.int32)
        column = slot & 127
        moved = HALF + (column & 1) * 32 + ((column - HALF) >> 1)
        lines_ref[0] = (slot >> 7).astype(F32)
        column = jnp.where(column < HALF, column, moved)
        lines_ref[1] = column.astype(F32)
        lines_ref[2] = ((slot >> 7) & 31).astype(F32)
        places = (column + ((slot >> 12) << 7)).astype(F32).T.astype(BF16)

        def tall(r):
            hit = repeated_row(lines_ref.at[0], r, 4) == row_iota
            first = [jnp.where(hit, repeated_row(parts_ref.at[i], r, 4), zero) for i in range(4)]
            place = repeated_row(lines_ref.at[1], r, 8) == column_iota
            return jnp.concatenate(first, axis=0), jnp.where(place, one, zero)

        def wide(r):
            hit = repeated_row(lines_ref.at[2], r, 2) == row_iota[:32]
            first = [jnp.where(hit, repeated_row(parts_ref.at[i], r, 2), zero) for i in range(4)]
            place = jnp.broadcast_to(places[:, r : r + 1], (LANES, 256)) == wide_iota
            return jnp.concatenate(first, axis=0), jnp.where(place, one, zero)

        dense = None
        other = None
        for r in range(0, 32, 2):
            if r % 4 == 2:
                pairs = [wide(r), wide(r + 1)]
                first = jnp.concatenate([pair[0] for pair in pairs], axis=1)
                term = dot(first, jnp.concatenate([pair[1] for pair in pairs], axis=0))
                other = term if other is None else other + term
            else:
                pairs = [tall(r), tall(r + 1)]
                first = jnp.concatenate([pair[0] for pair in pairs], axis=1)
                second = jnp.concatenate([pair[1] for pair in pairs], axis=1)
                term = lax.dot_general(
                    first, second, (((1,), (1,)), ((), ())), preferred_element_type=F32
                )
                dense = term if dense is None else dense + term
        real = dense[0:64] + dense[64:128]
        imag = dense[128:192] + dense[192:256]
        other_real = other[0:32] + other[32:64]
        other_imag = other[64:96] + other[96:128]
        real += jnp.concatenate([other_real[:, :LANES], other_real[:, LANES:]], axis=0)
        imag += jnp.concatenate([other_imag[:, :LANES], other_imag[:, LANES:]], axis=0)
        dense_ref[s] = jnp.concatenate([real, imag], axis=1)

    for s in range(8):
        scatter(s, parts_ref.at[s], lines_ref.at[s])

    y = []
    for s in range(8):
        high, low = split(dense_ref[s])
        v_high, v_low = split(v_rows(s))
        y.append(dot(v_high, high) + dot(v_high, low) + dot(v_low, high))
    def times(matrix, x):
        m_high, m_low = split(matrix)
        x_high, x_low = split(x)
        return dot(m_high, x_high) + dot(m_high, x_low) + dot(m_low, x_high)

    steps = []
    for s in range(8):
        source = jnp.concatenate([y[s][:, :HALF], y[s][:, LANES : LANES + HALF]], axis=0)
        couple_real = SCREEN * y[s][:, HALF:LANES]
        couple_imag = SCREEN * y[s][:, LANES + HALF :]
        matrix = jnp.concatenate(
            [
                jnp.concatenate([couple_real, -couple_imag], axis=1),
                jnp.concatenate([couple_imag, couple_real], axis=1),
            ],
            axis=0,
        )
        steps.append((matrix, source))
    x = [steps[0][1]]
    pairs = []
    for s in (1, 3, 5):
        joined = times(steps[s + 1][0], jnp.concatenate(steps[s], axis=1))
        pairs.append((joined[:, :LANES], joined[:, LANES:] + steps[s + 1][1]))
    for i, s in enumerate((1, 3, 5)):
        x.append(times(steps[s][0], x[s - 1]) + steps[s][1])
        x.append(times(pairs[i][0], x[s - 1]) + pairs[i][1])
    x.append(times(steps[7][0], x[6]) + steps[7][1])
    for s in range(8):
        for part in range(2):
            rows = x[s][part * HALF : (part + 1) * HALF]
            out_ref[s, part] = jnp.concatenate([rows[:32], rows[32:]], axis=1)


def tables(count):
    half = np.arange(count) + 0.5
    angle = np.outer(half, half) * (math.pi / count)
    table = np.concatenate([np.cos(angle), np.sin(angle)]).astype(np.float32)
    high = table.astype(jnp.bfloat16)
    low = (table - high.astype(np.float32)).astype(jnp.bfloat16)
    return np.concatenate([high, low]).reshape(4, count, count)


def vmem(n):
    return [pl.BlockSpec(memory_space=pltpu.VMEM)] * n


def pack(lesser, greater, v_blocks, slots):
    return pl.pallas_call(
        pack_kernel,
        out_shape=(
            pltpu.VMEM((64, 16, LANES), F32),
            pltpu.VMEM((8, LANES), F32),
            pltpu.VMEM((4, 512, 512), BF16),
        ),
        in_specs=[pl.BlockSpec(memory_space=pl.ANY)] * 5,
        out_specs=tuple(vmem(3)),
        scratch_shapes=[
            pltpu.VMEM((512, LANES), F32),
            pltpu.VMEM((512, LANES), F32),
            pltpu.VMEM((1, HALF, HALF), F32),
            pltpu.VMEM((32, LANES), jnp.int32),
            pltpu.SemaphoreType.DMA((8,)),
        ],
        name="pack",
    )(
        lesser.reshape(512, LANES),
        greater.reshape(512, LANES),
        jnp.asarray(tables(512)),
        v_blocks,
        slots.reshape(32, LANES),
    )


def correlate(data, side, table):
    return pl.pallas_call(
        correlate_kernel,
        out_shape=jax.ShapeDtypeStruct((1024, LANES), F32),
        in_specs=vmem(3),
        out_specs=vmem(1)[0],
        compiler_params=pltpu.CompilerParams(vmem_limit_bytes=40 << 20),
        name="correlate",
    )(data.reshape(64, 2, 8, LANES), side, table)


def screen(data):
    return pl.pallas_call(
        screen_kernel,
        out_shape=jax.ShapeDtypeStruct((8, 2, 32, LANES), F32),
        in_specs=vmem(1),
        out_specs=vmem(1)[0],
        scratch_shapes=[
            pltpu.VMEM((8, 4, 32, LANES), F32),
            pltpu.VMEM((8, 3, 32, LANES), F32),
            pltpu.VMEM((8, HALF, 256), F32),
        ],
        compiler_params=pltpu.CompilerParams(vmem_limit_bytes=40 << 20),
        name="screen",
    )(data)


def place_kernel(blocks_ref, out_hbm, sems):
    copies = []
    for part in range(2):
        for i in range(2):
            rows = pl.ds(4 * i, 4)
            copies.append(
                pltpu.make_async_copy(
                    blocks_ref.at[rows, part], out_hbm.at[part, rows], sems.at[part, i]
                )
            )
    for copy in copies:
        copy.start()
    for copy in copies:
        copy.wait()


def place(blocks):
    return pl.pallas_call(
        place_kernel,
        out_shape=jax.ShapeDtypeStruct((2, 8, 32, LANES), F32),
        in_specs=vmem(1),
        out_specs=pl.BlockSpec(memory_space=pl.ANY),
        scratch_shapes=[pltpu.SemaphoreType.DMA((2, 2))],
        name="place",
    )(pltpu.with_memory_space_constraint(blocks.reshape(8, 2, 32, LANES), pltpu.VMEM))


def shards(g_lesser, g_greater, v_blocks, slots):
    data, side, table = pack(g_lesser, g_greater, v_blocks, slots)
    data = lax.all_to_all(data.reshape(64, 1, 2048), "energy", 0, 0, tiled=True)
    data = correlate(data, side, table).reshape(512, 1, 256)
    data = lax.all_to_all(data, ("energy", "cuts"), 0, 0, tiled=True)
    blocks = screen(data.reshape(1024, LANES)).reshape(8, 64, LANES)
    blocks = lax.all_to_all(blocks, "cuts", 0, 0, tiled=True)
    return place(blocks).reshape(2, 8, 1, 4096)


def solution(mesh):
    placed = (
        P(None, "energy", "cuts", None),
        P(None, "energy", "cuts", None),
        P("cuts", None, None),
        P("cuts", None),
    )
    return jax.shard_map(
        shards,
        mesh=mesh,
        in_specs=placed,
        out_specs=P(None, "energy", "cuts", None),
        check_vma=False,
    )
```

```python
import functools
import math

import jax
import jax.numpy as jnp
import numpy as np
from jax import lax
from jax.experimental import pallas as pl
from jax.experimental.pallas import tpu as pltpu
from jax.sharding import PartitionSpec as P

SCREEN = 0.08
F32 = jnp.float32
BF16 = jnp.bfloat16
LANES = 128
HALF = 64


def split(x):
    high = x.astype(BF16)
    return high, (x - high.astype(F32)).astype(BF16)


def left_half(shape):
    return lax.broadcasted_iota(jnp.int32, shape, len(shape) - 1) < HALF


def dot(a, b):
    return jnp.dot(a, b, preferred_element_type=F32)


def pack_kernel(
    lesser_hbm, greater_hbm, table_hbm, v_hbm, slots_hbm, out_ref, side_ref, table_ref,
    lesser_ref, greater_ref, v_ref, slots_ref, sems,
):
    copies = [
        pltpu.make_async_copy(lesser_hbm, lesser_ref, sems.at[0]),
        pltpu.make_async_copy(greater_hbm, greater_ref, sems.at[1]),
    ]
    for i in range(4):
        copies.append(pltpu.make_async_copy(table_hbm.at[i], table_ref.at[i], sems.at[2 + i]))
    copies.append(pltpu.make_async_copy(v_hbm, v_ref, sems.at[6]))
    copies.append(pltpu.make_async_copy(slots_hbm, slots_ref, sems.at[7]))
    for copy in copies:
        copy.start()
    left = left_half((8, LANES))
    for which, ref in enumerate((lesser_ref, greater_ref)):
        copies[which].wait()
        for tile in range(32):
            real = ref[pl.ds(tile, 8, stride=32), :]
            imag = ref[pl.ds(256 + tile, 8, stride=32), :]
            rows = pl.ds(which * 8, 8)
            out_ref[2 * tile, rows, :] = jnp.where(left, real, pltpu.roll(imag, HALF, 1))
            out_ref[2 * tile + 1, rows, :] = jnp.where(left, pltpu.roll(real, HALF, 1), imag)
    for copy in copies[2:]:
        copy.wait()
    me = lax.axis_index("energy")
    slot = slots_ref[pl.ds(me // 2, 1), :].astype(F32)
    slot = jnp.where(me % 2 == 0, slot, pltpu.roll(slot, HALF, 1))[:, :HALF]
    side = jnp.concatenate([slot, v_ref[0, pl.ds(me, 1), :]], axis=1)
    side_ref[...] = jnp.broadcast_to(side, (8, LANES))


def correlate_kernel(data_ref, side_ref, table_ref, out_ref):
    count = 512
    left = left_half((count, LANES))
    sign = jnp.where(left, 1.0, -1.0).astype(F32)

    def turned(x):
        return pltpu.roll(x, HALF, 1)

    out_ref[pl.ds(1, count, stride=2), :] = jnp.broadcast_to(side_ref[pl.ds(0, 1), :], (count, LANES))

    lesser = data_ref[:, 0].reshape(count, LANES)
    greater = data_ref[:, 1].reshape(count, LANES)
    sig_high, sig_low = split(jnp.concatenate([lesser, greater], axis=1))
    both = jnp.concatenate([sig_high, sig_low], axis=1)
    cosines = dot(table_ref[0], both)
    sines = dot(table_ref[1], both)
    cosines = cosines[:, :256] + cosines[:, 256:] + dot(table_ref[2], sig_high)
    sines = sines[:, :256] + sines[:, 256:] + dot(table_ref[3], sig_high)
    cos_a, cos_b = cosines[:, :LANES], cosines[:, LANES:]
    sin_a, sin_b = sines[:, :LANES], sines[:, LANES:]
    shift_a, shift_b = sign * turned(sin_a), sign * turned(sin_b)

    def times_conjugate(a, b):
        other_b = turned(b)
        real_b = jnp.where(left, b, other_b)
        imag_b = jnp.where(left, other_b, b)
        return a * real_b + (sign * turned(a)) * imag_b

    plus = times_conjugate(cos_a + shift_a, cos_b + shift_b)
    minus = times_conjugate(cos_a - shift_a, cos_b - shift_b)
    for_cos = -sign * turned(plus + minus)
    for_sin = minus - plus
    scale = 1.0 / (2 * count * math.sqrt(count))

    def turn(i):
        column = table_ref[i, :, :LANES][:, :1].astype(F32)
        column += table_ref[i + 2, :, :LANES][:, :1].astype(F32)
        return jnp.broadcast_to(column * scale, (count, LANES))

    turn_cos, turn_sin = turn(0), turn(1)
    cos_high, cos_low = split(turn_cos * for_cos - turn_sin * for_sin)
    sin_high, sin_low = split(turn_sin * for_cos + turn_cos * for_sin)
    result = dot(table_ref[0], jnp.concatenate([cos_high, cos_low], axis=1))
    result += dot(table_ref[1], jnp.concatenate([sin_high, sin_low], axis=1))
    result = result[:, :LANES] + result[:, LANES:]
    result += dot(table_ref[2], cos_high) + dot(table_ref[3], sin_high)
    out_ref[pl.ds(0, count, stride=2), :] = result


def repeated_row(ref, row, times):
    tile = jnp.broadcast_to(ref[pl.ds(row, 1), :], (16, LANES)).astype(BF16)
    return jnp.concatenate([tile] * times, axis=0)


def screen_kernel(data_ref, out_ref, parts_ref, lines_ref, dense_ref):
    left32 = left_half((32, LANES))
    row_iota = lax.broadcasted_iota(jnp.int32, (HALF, LANES), 0).astype(F32).astype(BF16)
    column_iota = lax.broadcasted_iota(jnp.int32, (LANES, LANES), 0).astype(F32).astype(BF16)
    wide_iota = lax.broadcasted_iota(jnp.int32, (LANES, 256), 1).astype(F32).astype(BF16)
    zero = jnp.zeros((), BF16)
    one = jnp.ones((), BF16)

    def lines(s, side):
        return [data_ref[pl.ds(2 * s + side + 16 * odd, 32, stride=32), :] for odd in range(2)]

    def join(even, odd):
        return jnp.where(left32, even, pltpu.roll(odd, HALF, 1))

    def join_right(even, odd):
        return jnp.where(left32, pltpu.roll(even, HALF, 1), odd)

    def v_rows(s):
        return jnp.concatenate(lines(s, 1), axis=0)[:, HALF:]

    def scatter(s, parts_ref, lines_ref):
        polar = lines(s, 0)
        for i, part in enumerate((*split(join(*polar)), *split(join_right(*polar)))):
            parts_ref[i] = part.astype(F32)
        slot = join(*lines(s, 1)).astype(jnp.int32)
        column = slot & 127
        moved = HALF + (column & 1) * 32 + ((column - HALF) >> 1)
        lines_ref[0] = (slot >> 7).astype(F32)
        column = jnp.where(column < HALF, column, moved)
        lines_ref[1] = column.astype(F32)
        lines_ref[2] = ((slot >> 7) & 31).astype(F32)
        places = (column + ((slot >> 12) << 7)).astype(F32).T.astype(BF16)

        def tall(r):
            hit = repeated_row(lines_ref.at[0], r, 4) == row_iota
            first = [jnp.where(hit, repeated_row(parts_ref.at[i], r, 4), zero) for i in range(4)]
            place = repeated_row(lines_ref.at[1], r, 8) == column_iota
            return jnp.concatenate(first, axis=0), jnp.where(place, one, zero)

        def wide(r):
            hit = repeated_row(lines_ref.at[2], r, 2) == row_iota[:32]
            first = [jnp.where(hit, repeated_row(parts_ref.at[i], r, 2), zero) for i in range(4)]
            place = jnp.broadcast_to(places[:, r : r + 1], (LANES, 256)) == wide_iota
            return jnp.concatenate(first, axis=0), jnp.where(place, one, zero)

        dense = None
        other = None
        for r in range(0, 32, 2):
            if r % 16 in (2, 6, 8, 10, 14):
                pairs = [wide(r), wide(r + 1)]
                first = jnp.concatenate([pair[0] for pair in pairs], axis=1)
                term = dot(first, jnp.concatenate([pair[1] for pair in pairs], axis=0))
                other = term if other is None else other + term
            else:
                pairs = [tall(r), tall(r + 1)]
                first = jnp.concatenate([pair[0] for pair in pairs], axis=1)
                second = jnp.concatenate([pair[1] for pair in pairs], axis=1)
                term = lax.dot_general(
                    first, second, (((1,), (1,)), ((), ())), preferred_element_type=F32
                )
                dense = term if dense is None else dense + term
        real = dense[0:64] + dense[64:128]
        imag = dense[128:192] + dense[192:256]
        other_real = other[0:32] + other[32:64]
        other_imag = other[64:96] + other[96:128]
        real += jnp.concatenate([other_real[:, :LANES], other_real[:, LANES:]], axis=0)
        imag += jnp.concatenate([other_imag[:, :LANES], other_imag[:, LANES:]], axis=0)
        dense_ref[s] = jnp.concatenate([real, imag], axis=1)

    for s in range(8):
        scatter(s, parts_ref.at[s], lines_ref.at[s])

    y = []
    for s in range(8):
        high, low = split(dense_ref[s])
        v_high, v_low = split(v_rows(s))
        y.append(dot(v_high, high) + dot(v_high, low) + dot(v_low, high))
    def times(matrix, x):
        m_high, m_low = split(matrix)
        x_high, x_low = split(x)
        return dot(m_high, x_high) + dot(m_high, x_low) + dot(m_low, x_high)

    steps = []
    for s in range(8):
        source = jnp.concatenate([y[s][:, :HALF], y[s][:, LANES : LANES + HALF]], axis=0)
        couple_real = SCREEN * y[s][:, HALF:LANES]
        couple_imag = SCREEN * y[s][:, LANES + HALF :]
        matrix = jnp.concatenate(
            [
                jnp.concatenate([couple_real, -couple_imag], axis=1),
                jnp.concatenate([couple_imag, couple_real], axis=1),
            ],
            axis=0,
        )
        steps.append((matrix, source))
    x = [steps[0][1]]
    pairs = []
    for s in (1, 3, 5):
        joined = times(steps[s + 1][0], jnp.concatenate(steps[s], axis=1))
        pairs.append((joined[:, :LANES], joined[:, LANES:] + steps[s + 1][1]))
    for i, s in enumerate((1, 3, 5)):
        x.append(times(steps[s][0], x[s - 1]) + steps[s][1])
        x.append(times(pairs[i][0], x[s - 1]) + pairs[i][1])
    x.append(times(steps[7][0], x[6]) + steps[7][1])
    for s in range(8):
        for part in range(2):
            rows = x[s][part * HALF : (part + 1) * HALF]
            out_ref[s, part] = jnp.concatenate([rows[:32], rows[32:]], axis=1)


def tables(count):
    half = np.arange(count) + 0.5
    angle = np.outer(half, half) * (math.pi / count)
    table = np.concatenate([np.cos(angle), np.sin(angle)]).astype(np.float32)
    high = table.astype(jnp.bfloat16)
    low = (table - high.astype(np.float32)).astype(jnp.bfloat16)
    return np.concatenate([high, low]).reshape(4, count, count)


def vmem(n):
    return [pl.BlockSpec(memory_space=pltpu.VMEM)] * n


def pack(lesser, greater, v_blocks, slots):
    return pl.pallas_call(
        pack_kernel,
        out_shape=(
            pltpu.VMEM((64, 16, LANES), F32),
            pltpu.VMEM((8, LANES), F32),
            pltpu.VMEM((4, 512, 512), BF16),
        ),
        in_specs=[pl.BlockSpec(memory_space=pl.ANY)] * 5,
        out_specs=tuple(vmem(3)),
        scratch_shapes=[
            pltpu.VMEM((512, LANES), F32),
            pltpu.VMEM((512, LANES), F32),
            pltpu.VMEM((1, HALF, HALF), F32),
            pltpu.VMEM((32, LANES), jnp.int32),
            pltpu.SemaphoreType.DMA((8,)),
        ],
        name="pack",
    )(
        lesser.reshape(512, LANES),
        greater.reshape(512, LANES),
        jnp.asarray(tables(512)),
        v_blocks,
        slots.reshape(32, LANES),
    )


def correlate(data, side, table):
    return pl.pallas_call(
        correlate_kernel,
        out_shape=jax.ShapeDtypeStruct((1024, LANES), F32),
        in_specs=vmem(3),
        out_specs=vmem(1)[0],
        compiler_params=pltpu.CompilerParams(vmem_limit_bytes=40 << 20),
        name="correlate",
    )(data.reshape(64, 2, 8, LANES), side, table)


def screen(data):
    return pl.pallas_call(
        screen_kernel,
        out_shape=jax.ShapeDtypeStruct((8, 2, 32, LANES), F32),
        in_specs=vmem(1),
        out_specs=vmem(1)[0],
        scratch_shapes=[
            pltpu.VMEM((8, 4, 32, LANES), F32),
            pltpu.VMEM((8, 3, 32, LANES), F32),
            pltpu.VMEM((8, HALF, 256), F32),
        ],
        compiler_params=pltpu.CompilerParams(vmem_limit_bytes=40 << 20),
        name="screen",
    )(data)


def place_kernel(blocks_ref, out_hbm, sems):
    copies = []
    for part in range(2):
        for i in range(2):
            rows = pl.ds(4 * i, 4)
            copies.append(
                pltpu.make_async_copy(
                    blocks_ref.at[rows, part], out_hbm.at[part, rows], sems.at[part, i]
                )
            )
    for copy in copies:
        copy.start()
    for copy in copies:
        copy.wait()


def place(blocks):
    return pl.pallas_call(
        place_kernel,
        out_shape=jax.ShapeDtypeStruct((2, 8, 32, LANES), F32),
        in_specs=vmem(1),
        out_specs=pl.BlockSpec(memory_space=pl.ANY),
        scratch_shapes=[pltpu.SemaphoreType.DMA((2, 2))],
        name="place",
    )(pltpu.with_memory_space_constraint(blocks.reshape(8, 2, 32, LANES), pltpu.VMEM))


def shards(g_lesser, g_greater, v_blocks, slots):
    data, side, table = pack(g_lesser, g_greater, v_blocks, slots)
    data = lax.all_to_all(data.reshape(64, 1, 2048), "energy", 0, 0, tiled=True)
    data = correlate(data, side, table).reshape(512, 1, 256)
    data = lax.all_to_all(data, ("energy", "cuts"), 0, 0, tiled=True)
    blocks = screen(data.reshape(1024, LANES)).reshape(8, 64, LANES)
    blocks = lax.all_to_all(blocks, "cuts", 0, 0, tiled=True)
    return place(blocks).reshape(2, 8, 1, 4096)


def solution(mesh):
    placed = (
        P(None, "energy", "cuts", None),
        P(None, "energy", "cuts", None),
        P("cuts", None, None),
        P("cuts", None),
    )
    return jax.shard_map(
        shards,
        mesh=mesh,
        in_specs=placed,
        out_specs=P(None, "energy", "cuts", None),
        check_vma=False,
    )
```
